32 devices in a mesh: fsdp: 2 (over y), ctx: 4 (over z), tp: 4 (over x, core).
Axes of the slice: x: 2, y: 2, z: 4, core: 2. Of those that a mesh axis runs over, the one named last changes fastest.
Arguments:
- hidden: bfloat16 [8192, 768], P(('fsdp', 'ctx', 'tp')), may hold values from -6 to 6
- latent: bfloat16 [8192, 768], P(('fsdp', 'ctx', 'tp')), may hold values from -8 to 8
- latent_mask: int32 [8192], P(('fsdp', 'ctx', 'tp')), may hold values 0 or 1
- segment_ids: int32 [2, 4096], P('fsdp'), may hold values from 0 to 31, never falling along the last dimension, each value on 1 to 800 neighbouring positions
- norm_gains: bfloat16 [2, 768], replicated, may hold values from 0.25 to 1.75
- row_biases: bfloat16 [4, 768], replicated, may hold values from -3 to 3
- qv_bias: bfloat16 [2, 768], P(None, 'tp'), may hold values from -3 to 3
- fc_bias: bfloat16 [3072], P('tp'), may hold values from -3 to 3
- w_qkv: bfloat16 [3, 768, 768], P(None, 'tp', 'fsdp'), may hold values from -0.21875 to 0.21875
- w_out: bfloat16 [768, 768], P('tp', 'fsdp'), may hold values from -0.875 to 0.875
- w_fc: bfloat16 [3072, 768], P('tp', 'fsdp'), may hold values from -0.21875 to 0.21875
- w_proj: bfloat16 [3072, 768], P('tp', 'fsdp'), may hold values from -0.15625 to 0.15625
- cotangent: bfloat16 [8192, 768], P(('fsdp', 'ctx', 'tp')), may hold values from -6 to 6
Outputs:
- block_out: bfloat16 [8192, 768], P(('fsdp', 'ctx', 'tp'))
- grad_input: bfloat16 [8192, 768], P(('fsdp', 'ctx', 'tp'))
- grad_w_qkv: float32 [3, 768, 768], P(None, 'tp', 'fsdp')
- grad_w_out: float32 [768, 768], P('tp', 'fsdp')
- grad_w_fc: float32 [3072, 768], P('tp', 'fsdp')
- grad_w_proj: float32 [3072, 768], P('tp', 'fsdp')
- grad_gains: float32 [2, 768], P(None, 'tp')
- grad_row_biases: float32 [4, 768], P(None, 'tp')
- grad_qv_bias: float32 [2, 768], P(None, 'tp')
- grad_fc_bias: float32 [3072], P('tp')
The draws below stay inside these ranges and needn't reach their ends.
Inputs may be any that keep to these rules, and one draw needn't show every extreme that they name: `segment_ids`: along each row the document ids never fall; each document covers 1 to 800 positions and one covers exactly 800.
All inputs are finite; a program needn't handle non-finite values. No bound on the sum of `latent_mask` on one device may be relied on, other than what follows from the above.
Results may differ from the reference program's by a relative error of at most 0.017.
Values may be sent and summed in bfloat16 or wider, within the bound.
No kernel may reach another device: no remote copies, remote signals or barrier semaphores. Data moves between devices by JAX's collectives and lax.ppermute only.
A program may use at most 128 MiB of HBM per device.

```python
import math
import jax
import jax.numpy as jnp
import numpy as np
from jax import lax

D = 768
HEADS = 12
HEAD = 64
FF = 3072
LEN = 4096
DOC_MOST = 800
DOCS = 32
SEQS = 2
TOKENS = 8192


def place_ends(entries, key, least, high):
    longest = entries.shape.index(max(entries.shape))
    spots = []
    for shift in (0, 1):
        where = [jax.random.randint(jax.random.fold_in(key, axis), (), 0, length) for axis, length in enumerate(entries.shape)]
        where[longest] = (where[longest] + shift) % entries.shape[longest]
        spots.append(tuple(where))
    return entries.at[spots[0]].set(least).at[spots[1]].set(high)


def shard_levels(stream_key, dims, cuts, least, high):
    loudness, own = 1.0, jax.random.fold_in(stream_key, 6)
    for axis_at, parts in cuts:
        steps = jnp.exp(jax.random.uniform(jax.random.fold_in(own, axis_at), (parts,), jnp.float32, least / len(cuts), high / len(cuts)))
        loudness = loudness * jnp.repeat(steps, dims[axis_at] // parts).reshape([-1 if axis == axis_at else 1 for axis in range(len(dims))])
    return loudness


def length_profile(number_of, total, reach, slope):
    loads = [(1 << 20) // math.isqrt(rank ** slope) + 1 for rank in range(2, number_of + 1)]
    spare, given = total - reach - (number_of - 1), [1] * (number_of - 1)
    while spare > 0:
        candidates = [i for i in range(number_of - 1) if given[i] < reach]
        whole, left = sum([loads[i] for i in candidates]), spare
        for i in candidates:
            extra = min(reach - given[i], max(1, left * loads[i] // whole), spare)
            given[i] = given[i] + extra
            spare = spare - extra
    return np.array([reach] + given)


def ragged_sizes(own_key, count, total, most, lean):
    if count == 2:
        one = jax.random.randint(own_key, (), max(1, total - most), min(most, total - 1) + 1)
        return jnp.stack([one, total - one])
    lengths = jnp.asarray(length_profile(count, total, most, lean), jnp.int32)
    pairs = (count - 1) // 2
    source_of, receiver = lengths[1:1 + 2 * pairs:2], lengths[2:2 + 2 * pairs:2]
    margin = jnp.minimum(source_of - 1, most - receiver)
    moved = jax.random.randint(jax.random.fold_in(own_key, 1), (pairs,), 0, 1 << 20) % (margin + 1)
    lengths = lengths.at[1:1 + 2 * pairs:2].set(source_of - moved).at[2:2 + 2 * pairs:2].set(receiver + moved)
    return lengths[jax.random.permutation(jax.random.fold_in(own_key, 2), count)]


def gaussian(stream_key, shape, deviation, most, pieces=(), kind=jnp.bfloat16):
    entries = deviation * jax.random.normal(stream_key, shape, jnp.float32)
    if pieces:
        entries = entries * shard_levels(stream_key, shape, pieces, -0.22, 0.18)
    return jnp.clip(entries, -most, most).astype(kind)


def setup_inputs(seed: int = 0) -> dict:
    streams_of = jax.random.split(jax.random.key(seed), 14)
    hidden = gaussian(streams_of[0], (TOKENS, D), 1.0, 6.0, ((0, 32),))
    latent = gaussian(streams_of[1], (TOKENS, D), 1.5, 8.0, ((0, 32),))
    latent_mask = place_ends((jax.random.randint(streams_of[2], (TOKENS,), 0, 6) < 1).astype(jnp.int32), jax.random.fold_in(streams_of[2], 1), 0, 1)
    segment_ids = jax.vmap(lambda own: jnp.searchsorted(jnp.cumsum(ragged_sizes(own, DOCS, LEN, DOC_MOST, 2)), jnp.arange(LEN), side="right"))(jax.random.split(streams_of[3], SEQS)).reshape((SEQS, LEN)).astype(jnp.int32)
    norm_gains = jnp.clip(1.0 + 0.15 * jax.random.normal(streams_of[4], (2, D), jnp.float32), 0.25, 1.75).astype(jnp.bfloat16)
    row_biases = gaussian(streams_of[5], (4, D), 0.5, 3.0)
    qv_bias = gaussian(streams_of[6], (2, D), 0.5, 3.0, ((1, 4),))
    fc_bias = gaussian(streams_of[7], (FF,), 0.5, 3.0, ((0, 4),))
    w_qkv = gaussian(streams_of[8], (3, D, D), D ** -0.5, 0.21875, ((1, 4), (2, 2)))
    w_out = gaussian(streams_of[9], (D, D), (D // 16) ** -0.5, 0.875, ((0, 4), (1, 2)))
    w_fc = gaussian(streams_of[10], (FF, D), D ** -0.5, 0.21875, ((0, 4), (1, 2)))
    w_proj = gaussian(streams_of[11], (FF, D), (FF // 2) ** -0.5, 0.15625, ((0, 4), (1, 2)))
    cotangent = gaussian(streams_of[12], (TOKENS, D), 1.0, 6.0, ((0, 32),))
    return {"hidden": hidden, "latent": latent, "latent_mask": latent_mask, "segment_ids": segment_ids, "norm_gains": norm_gains, "row_biases": row_biases, "qv_bias": qv_bias, "fc_bias": fc_bias, "w_qkv": w_qkv, "w_out": w_out, "w_fc": w_fc, "w_proj": w_proj, "cotangent": cotangent}


@jax.custom_vjp
def low(v):
    return lax.optimization_barrier(v.astype(jnp.bfloat16)).astype(jnp.float32)

@jax.custom_vjp
def low_back(v):
    return v

def low_keep(v):
    return (low(v), None)

def low_pass(kept, grad):
    return (grad,)

def back_keep(v):
    return (v, None)

def back_low(kept, grad):
    return (low(grad),)
low.defvjp(low_keep, low_pass)
low_back.defvjp(back_keep, back_low)

def matmul(left, right):
    return jnp.dot(left, right, precision=lax.Precision.HIGHEST)

def matmul_trans(left, right):
    return jnp.dot(left, right.T, precision=lax.Precision.HIGHEST)

def normalize(values, gain, shift):
    mean = lax.optimization_barrier(jnp.mean(values, axis=-1, keepdims=True))
    centered = values - mean
    variance = lax.optimization_barrier(jnp.mean(centered * centered, axis=-1, keepdims=True))
    return centered * lax.rsqrt(variance + 1e-05) * gain + shift

def sequence_attention(packed):
    queries, keys, values, segments = packed
    position = jnp.arange(LEN, dtype=jnp.int32)
    allowed = (position[None, :] <= position[:, None]) & (segments[None, :] == segments[:, None])
    scores = jnp.einsum('qhd,khd->hqk', queries, keys, precision=lax.Precision.HIGHEST) * HEAD ** (-0.5)
    scores = low_back(scores)
    scores = jnp.where(allowed[None], scores, -1e+30)
    highest = lax.optimization_barrier(jnp.max(scores, axis=-1, keepdims=True))
    log_total = highest + jnp.log(lax.optimization_barrier(jnp.sum(jnp.exp(scores - highest), axis=-1, keepdims=True)))
    weights = low(jnp.exp(scores - log_total))
    mixed = jnp.einsum('hqk,khd->qhd', weights, values, precision=lax.Precision.HIGHEST)
    return mixed.reshape(LEN, HEADS * HEAD)

def reference(hidden, latent, latent_mask, segment_ids, norm_gains, row_biases, qv_bias, fc_bias, w_qkv, w_out, w_fc, w_proj, cotangent):
    chosen = (latent_mask == 1)[:, None]
    attention_step = jax.checkpoint(sequence_attention)

    def forward(hid, lat, gains, biases, qvb, fcb, wqkv, wout, wfc, wproj):
        start = jnp.where(chosen, lat, hid)
        norm_one = low(normalize(start, gains[0], biases[0]))
        queries = low(low_back(matmul_trans(norm_one, wqkv[0]) + qvb[0]))
        keys = low(low_back(matmul_trans(norm_one, wqkv[1])))
        values = low(low_back(matmul_trans(norm_one, wqkv[2]) + qvb[1]))
        shaped = lambda arr: arr.reshape(SEQS, LEN, HEADS, HEAD)
        mixed = lax.map(attention_step, (shaped(queries), shaped(keys), shaped(values), segment_ids))
        mixed = low(low_back(mixed.reshape(SEQS * LEN, HEADS * HEAD)))
        branch = low_back(matmul(mixed, wout))
        resid = start + branch + biases[2]
        norm_two = low(normalize(low(resid), gains[1], biases[1]))
        pre_act = low_back(matmul_trans(norm_two, wfc) + fcb)
        activ = low(jax.nn.gelu(pre_act, approximate=True))
        ffn_out = low_back(matmul(activ, wproj))
        return resid + ffn_out + biases[3]
    inputs = tuple((item.astype(jnp.float32) for item in (hidden, latent, norm_gains, row_biases, qv_bias, fc_bias, w_qkv, w_out, w_fc, w_proj)))
    result, pullback = jax.vjp(forward, *inputs)
    grads = pullback(cotangent.astype(jnp.float32))
    grad_in = grads[0] + grads[1]
    return (result.astype(jnp.bfloat16), grad_in.astype(jnp.bfloat16), grads[6], grads[7], grads[8], grads[9], grads[2], grads[3], grads[4], grads[5])
```

```python
from functools import partial

import jax
import jax.numpy as jnp
from jax import lax
from jax.experimental import pallas as pl
from jax.experimental.pallas import tpu as pltpu
from jax.sharding import PartitionSpec as P

HEAD = 64
TILE = 256
epsilon = 1e-05
masked_score = -1e30
f32 = jnp.float32
bf16 = jnp.bfloat16

ANY = pl.BlockSpec(memory_space=pl.ANY)
VM = pl.BlockSpec(memory_space=pltpu.VMEM)
SM = pl.BlockSpec(memory_space=pltpu.SMEM)


def nn(a, b):
    return lax.dot_general(a, b, (((1,), (0,)), ((), ())), preferred_element_type=f32)


def nt(a, b):
    return lax.dot_general(a, b, (((1,), (1,)), ((), ())), preferred_element_type=f32)


def tn(a, b):
    return lax.dot_general(a, b, (((0,), (0,)), ((), ())), preferred_element_type=f32)


def call(body, outs, specs, scratch, name):
    return pl.pallas_call(
        body,
        out_shape=[jax.ShapeDtypeStruct(s, d) for s, d in outs],
        in_specs=specs,
        out_specs=[VM] * len(outs),
        scratch_shapes=scratch,
        name=name,
    )


def copies(pairs, sems, base=0):
    made = []
    for i, (src, dst) in enumerate(pairs):
        made.append(pltpu.make_async_copy(src, dst, sems.at[base + i]))
    for one in made:
        one.start()
    return made


def weight_pairs(parts, dst, side):
    if len(parts) == 1:
        return [(parts[0], dst)]
    width = parts[0].shape[1]
    mine = pl.multiple_of(side * width, 128)
    other = pl.multiple_of((1 - side) * width, 128)
    return [(parts[0], dst.at[:, pl.ds(mine, width)]), (parts[1], dst.at[:, pl.ds(other, width)])]


def norm_rows(values, gain, shift):
    mean = jnp.mean(values, axis=-1, keepdims=True)
    centered = values - mean
    variance = jnp.mean(centered * centered, axis=-1, keepdims=True)
    inverse = lax.rsqrt(variance + epsilon)
    unit = centered * inverse
    return unit * gain + shift, unit, inverse


def rows_of(tp, j, rows):
    return pl.multiple_of(lax.bitwise_xor(tp, j) * rows, rows)


def project_body(n_parts, halo, *refs):
    meta, gains, biases, qvb = refs[:4]
    xs = refs[4:8]
    parts = refs[8 : 8 + n_parts]
    outs = refs[8 + n_parts :]
    if halo:
        n1, unit, k, v, vt, xbuf, wbuf, sems = outs
    else:
        n1, unit, q, k, v, vt, xbuf, wbuf, sems = outs
    width = k.shape[1]
    rows = xs[0].shape[0]
    tp, side = meta[0], meta[1]
    wcopies = copies(weight_pairs(parts, wbuf, side), sems)
    xcopies = copies([(xs[j], xbuf.at[j]) for j in range(4)], sems, 2)
    gain = gains[0:1, :].astype(f32)
    shift = biases[0:1, :].astype(f32)
    bias_q = qvb[0:1, :].astype(f32)
    bias_v = qvb[1:2, :].astype(f32)
    bias_vt = jnp.transpose(jnp.broadcast_to(bias_v, (128, width)))[:, 0:1]
    for j in range(4):
        xcopies[j].wait()
        normed, unit_rows, _ = norm_rows(xbuf[j].astype(f32), gain, shift)
        low = normed.astype(bf16)
        r = pl.ds(rows_of(tp, j, rows), rows)
        n1[r, :] = low
        unit[r, :] = unit_rows.astype(bf16)
        if j == 0:
            for one in wcopies:
                one.wait()
        if not halo:
            q[r, :] = ((nt(low, wbuf[0:width, :]) + bias_q).astype(bf16) * 0.125).astype(bf16)
        k[r, :] = nt(low, wbuf[width : 2 * width, :]).astype(bf16)
        v[r, :] = (nt(low, wbuf[2 * width :, :]) + bias_v).astype(bf16)
        vt[:, r] = (nt(wbuf[2 * width :, :], low) + bias_vt).astype(bf16)


def project(halo, meta, gains, biases, qvb, xs, parts):
    rows, dim = xs[0].shape
    width = parts[0].shape[0] // 3
    total = 4 * rows
    outs = [((total, dim), bf16), ((total, dim), bf16)]
    if not halo:
        outs.append(((total, width), bf16))
    outs += [((total, width), bf16), ((total, width), bf16), ((width, total), bf16)]
    return call(
        partial(project_body, len(parts), halo),
        outs,
        [SM, VM, VM, VM] + [ANY] * (4 + len(parts)),
        [
            pltpu.VMEM((4, rows, dim), bf16),
            pltpu.VMEM((3 * width, dim), bf16),
            pltpu.SemaphoreType.DMA((6,)),
        ],
        "project_halo" if halo else "project_own",
    )(meta, gains, biases, qvb, *xs, *parts)


def lane_masks():
    lane = lax.broadcasted_iota(jnp.int32, (1, 128), 1)
    low = jnp.where(lane < HEAD, 1.0, 0.0).astype(bf16)
    return low, (1.0 - low.astype(f32)).astype(bf16)


def head_views(block, masks):
    pair = block[:, 0:128]
    return (pair * masks[0], pair * masks[1], block[:, 128:192])


def scores_of(k_pair, k_last, q_views, allowed):
    sides = (nt(k_pair, q_views[0]), nt(k_pair, q_views[1]), nt(k_last, q_views[2]))
    return [jnp.where(allowed, one, masked_score) for one in sides]


def allowed_in(jt, i, doc_row, own_tiles):
    key = jt * TILE + lax.broadcasted_iota(jnp.int32, (TILE, TILE), 0)
    query = (own_tiles + i) * TILE + lax.broadcasted_iota(jnp.int32, (1, TILE), 1)
    return (key >= doc_row) & (key <= query)


def attend_body(n_parts, *refs):
    meta, doc, q, k, v, vt, kh, vh, vth = refs[:9]
    parts = refs[9 : 9 + n_parts]
    a0, a1, a2, a3, ot, lse, wbuf, sems = refs[9 + n_parts :]
    tp, side = meta[0], meta[1]
    total, width = q.shape
    own_tiles = total // TILE
    wcopies = copies(weight_pairs(parts, wbuf, side), sems)
    masks = lane_masks()

    def q_block(i, _):
        r = pl.ds(pl.multiple_of(i * TILE, TILE), TILE)
        q_views = head_views(q[r, :], masks)
        doc_row = doc[0:1, r]
        start = (
            tuple(jnp.full((1, TILE), masked_score, f32) for _ in range(3)),
            tuple(jnp.zeros((1, TILE), f32) for _ in range(3)),
            tuple(jnp.zeros((HEAD, TILE), f32) for _ in range(3)),
        )

        def tile_step(jt, base, kk, vv, carry):
            rk = pl.ds(pl.multiple_of((jt - base) * TILE, TILE), TILE)
            highs, sums, accs = carry
            sides = scores_of(
                kk[rk, 0:128], kk[rk, 128:192], q_views, allowed_in(jt, i, doc_row, own_tiles)
            )
            new_h, new_s, new_a = [], [], []
            for h in range(3):
                high = jnp.maximum(highs[h], jnp.max(sides[h], axis=0, keepdims=True))
                shrink = jnp.exp(highs[h] - high)
                p = jnp.exp(sides[h] - high)
                new_h.append(high)
                new_s.append(sums[h] * shrink + jnp.sum(p, axis=0, keepdims=True))
                vv_h = vv[h * HEAD : (h + 1) * HEAD, rk]
                new_a.append(accs[h] * shrink + nn(vv_h, p.astype(bf16)))
            return tuple(new_h), tuple(new_s), tuple(new_a)

        low = meta[4 + i]
        carry = lax.fori_loop(
            low, own_tiles, lambda jt, cc: tile_step(jt, 0, kh, vth, cc), start
        )
        carry = lax.fori_loop(
            jnp.maximum(low, own_tiles),
            own_tiles + i + 1,
            lambda jt, cc: tile_step(jt, own_tiles, k, vt, cc),
            carry,
        )
        highs, sums, accs = carry
        for h in range(3):
            ot[h * HEAD : (h + 1) * HEAD, r] = (accs[h] / sums[h]).astype(bf16)
            lse[h : h + 1, r] = highs[h] + jnp.log(sums[h])
        return 0

    lax.fori_loop(0, own_tiles, q_block, 0)
    for one in wcopies:
        one.wait()
    rows = a0.shape[0]
    for j, out in ((3, a3), (1, a1), (2, a2), (0, a0)):
        r = pl.ds(rows_of(tp, j, rows), rows)
        out[...] = tn(ot[:, r], wbuf[...]).astype(bf16)


def attend(meta, doc, q, k, v, vt, kh, vh, vth, parts, dim):
    total, width = q.shape
    rows = total // 4
    outs = [((rows, dim), bf16)] * 4 + [((width, total), bf16), ((8, total), f32)]
    return call(
        partial(attend_body, len(parts)),
        outs,
        [SM] + [VM] * 8 + [ANY] * len(parts),
        [pltpu.VMEM((width, dim), bf16), pltpu.SemaphoreType.DMA((2,))],
        "attend",
    )(meta, doc, q, k, v, vt, kh, vh, vth, *parts)


def resid_body(x, a0, ac, ax, gains, biases, h_out, n2_out):
    h = (
        x[...].astype(f32)
        + (a0[...].astype(f32) + ac[...].astype(f32) + ax[...].astype(f32))
        + biases[2:3, :].astype(f32)
    )
    h_out[...] = h
    normed, _, _ = norm_rows(
        h.astype(bf16).astype(f32), gains[1:2, :].astype(f32), biases[1:2, :].astype(f32)
    )
    n2_out[...] = normed.astype(bf16)


def residual(x, a0, ac, ax, gains, biases):
    rows, dim = x.shape
    return call(
        resid_body, [((rows, dim), f32), ((rows, dim), bf16)], [VM] * 6, [], "residual"
    )(x, a0, ac, ax, gains, biases)


def ffn_kernel(n_parts, *refs):
    meta, fcb = refs[:2]
    n2s = refs[2:6]
    dys = refs[6:10]
    fcs = refs[10 : 10 + n_parts]
    projs = refs[10 + n_parts : 10 + 2 * n_parts]
    d0, d1, d2, d3, act, du, n2, dy, fcsum, fcw, pjw, sems = refs[10 + 2 * n_parts :]
    side = meta[1]
    rows = n2s[0].shape[0]
    wc = copies(weight_pairs(fcs, fcw, side), sems)
    pc = copies(weight_pairs(projs, pjw, side), sems, 2)
    nc = copies([(n2s[j], n2.at[pl.ds(j * rows, rows), :]) for j in range(4)], sems, 4)
    dc = copies([(dys[j], dy.at[pl.ds(j * rows, rows), :]) for j in range(4)], sems, 8)
    bias = fcb[...].astype(f32)
    for one in wc + pc + dc:
        one.wait()
    outs = (d0, d1, d2, d3)
    sums = jnp.zeros((1, fcw.shape[0]), f32)
    c0 = 0.7978845608028654
    c1 = 0.044715
    for j in range(4):
        r = pl.ds(j * rows, rows)
        nc[j].wait()
        u = nt(n2[r, :], fcw[...]) + bias
        sq = u * u
        th = jnp.tanh(c0 * u * (1.0 + c1 * sq))
        half = 0.5 * (1.0 + th)
        act[r, :] = (u * half).astype(bf16)
        slope = half + (0.5 * c0) * u * (1.0 - th * th) * (1.0 + (3.0 * c1) * sq)
        grad = (nt(dy[r, :], pjw[...]) * slope).astype(bf16)
        du[r, :] = grad
        sums = sums + jnp.sum(grad.astype(f32), axis=0, keepdims=True)
        outs[j][...] = nn(grad, fcw[...]).astype(bf16)
    fcsum[...] = sums


def ffn(meta, fcb, n2s, dys, fcs, projs):
    rows, dim = n2s[0].shape
    hidden = fcs[0].shape[0]
    total = 4 * rows
    outs = [((rows, dim), bf16)] * 4
    outs += [((total, hidden), bf16)] * 2 + [((total, dim), bf16)] * 2 + [((1, hidden), f32)]
    return call(
        partial(ffn_kernel, len(fcs)),
        outs,
        [SM, VM] + [ANY] * (8 + 2 * len(fcs)),
        [
            pltpu.VMEM((hidden, dim), bf16),
            pltpu.VMEM((hidden, dim), bf16),
            pltpu.SemaphoreType.DMA((12,)),
        ],
        "ffn",
    )(meta, fcb, *n2s, *dys, *fcs, *projs)


def halves(side, split, width):
    if not split:
        return [pl.ds(0, width)]
    part = width // 2
    return [
        pl.ds(pl.multiple_of(side * part, 128), part),
        pl.ds(pl.multiple_of((1 - side) * part, 128), part),
    ]


def ffn_grads_kernel(split, meta, act, du, n2, dy, *outs):
    side = meta[1]
    picks = halves(side, split, n2.shape[1])
    n = len(picks)
    for pick, out in zip(picks[::-1], outs[:n][::-1]):
        out[...] = tn(act[...], dy[:, pick]).astype(bf16)
    for pick, out in zip(picks[::-1], outs[n:][::-1]):
        out[...] = tn(du[...], n2[:, pick]).astype(bf16)


def ffn_grads(meta, act, du, n2, dy, split):
    hidden, dim = act.shape[1], n2.shape[1]
    n = 2 if split else 1
    outs = [((hidden, dim // n), bf16)] * (2 * n)
    return call(partial(ffn_grads_kernel, split), outs, [SM] + [VM] * 4, [], "ffn_grads")(
        meta, act, du, n2, dy
    )


def ffn_out_kernel(n_parts, *refs):
    meta, act = refs[:2]
    parts = refs[2 : 2 + n_parts]
    outs = refs[2 + n_parts : 6 + n_parts]
    pjw, sems = refs[6 + n_parts :]
    for one in copies(weight_pairs(parts, pjw, meta[1]), sems):
        one.wait()
    rows = outs[0].shape[0]
    for j in range(4):
        outs[j][...] = nn(act[pl.ds(j * rows, rows), :], pjw[...]).astype(bf16)


def ffn_out(meta, act, parts):
    total, hidden = act.shape
    dim = parts[0].shape[1] * len(parts)
    return call(
        partial(ffn_out_kernel, len(parts)),
        [((total // 4, dim), bf16)] * 4,
        [SM, VM] + [ANY] * len(parts),
        [pltpu.VMEM((hidden, dim), bf16), pltpu.SemaphoreType.DMA((2,))],
        "ffn_out",
    )(meta, act, *parts)


def norm_back(grad, unit, inverse, gain):
    g = grad * gain
    first = jnp.mean(g, axis=-1, keepdims=True)
    second = jnp.mean(g * unit, axis=-1, keepdims=True)
    return inverse * (g - first - unit * second)


def back_two_body(h, dy, d0, dc, dx, gains, dh_out, dhb_out, sums):
    dn = d0[...].astype(f32) + dc[...].astype(f32) + dx[...].astype(f32)
    gain = gains[1:2, :].astype(f32)
    _, unit, inverse = norm_rows(h[...].astype(bf16).astype(f32), gain, 0.0)
    grad = dy[...].astype(f32)
    dh = grad + norm_back(dn, unit, inverse, gain)
    dh_out[...] = dh
    dhb_out[...] = dh.astype(bf16)
    sums[...] = jnp.zeros_like(sums)
    sums[0:1, :] = jnp.sum(dn * unit, axis=0, keepdims=True)
    sums[1:2, :] = jnp.sum(dn, axis=0, keepdims=True)
    sums[2:3, :] = jnp.sum(dh, axis=0, keepdims=True)
    sums[3:4, :] = jnp.sum(grad, axis=0, keepdims=True)


def back_two(h, dy, d0, dc, dx, gains):
    rows, dim = h.shape
    outs = [((rows, dim), f32), ((rows, dim), bf16), ((8, dim), f32)]
    return call(back_two_body, outs, [VM] * 6, [], "back_two")(h, dy, d0, dc, dx, gains)


def attend_back_body(n_parts, *refs):
    meta, doc, q, k, v, kh, vh, ot, lse = refs[:9]
    ds_in = refs[9:13]
    parts = refs[13 : 13 + n_parts]
    dq, dk, dv, dkh, dvh, dhb, qvsum, wbuf, ka, va, kha, vha, sems = refs[13 + n_parts :]
    tp, side = meta[0], meta[1]
    total, width = q.shape
    rows = ds_in[0].shape[0]
    own_tiles = total // TILE
    wcopies = copies(weight_pairs(parts, wbuf, side), sems)
    dcopies = copies(
        [(ds_in[j], dhb.at[pl.ds(rows_of(tp, j, rows), rows), :]) for j in range(4)], sems, 2
    )
    masks = lane_masks()
    for acc in (ka, va, kha, vha):
        acc[...] = jnp.zeros_like(acc)
    for one in wcopies + dcopies:
        one.wait()

    def q_block(i, _):
        r = pl.ds(pl.multiple_of(i * TILE, TILE), TILE)
        q_views = head_views(q[r, :], masks)
        doc_row = doc[0:1, r]
        grad = nt(dhb[r, :], wbuf[...]).astype(bf16)
        grad_t = nt(wbuf[...], dhb[r, :]).astype(bf16).astype(f32)
        inner = ot[:, r].astype(f32) * grad_t
        deltas = [
            jnp.sum(inner[h * HEAD : (h + 1) * HEAD, :], axis=0, keepdims=True) for h in range(3)
        ]
        logs = [lse[h : h + 1, r] for h in range(3)]
        g_views = head_views(grad, masks)

        def tile_step(jt, base, kk, vv, kacc, vacc, carry):
            rk = pl.ds(pl.multiple_of((jt - base) * TILE, TILE), TILE)
            dq_pair, dq_last = carry
            k_pair, k_last = kk[rk, 0:128], kk[rk, 128:192]
            v_pair, v_last = vv[rk, 0:128], vv[rk, 128:192]
            sides = scores_of(k_pair, k_last, q_views, allowed_in(jt, i, doc_row, own_tiles))
            grads = (nt(v_pair, g_views[0]), nt(v_pair, g_views[1]), nt(v_last, g_views[2]))
            ps = [jnp.exp(sides[h] - logs[h]) for h in range(3)]
            low = [p.astype(bf16) for p in ps]
            dss = [(ps[h] * (grads[h] - deltas[h])).astype(bf16) for h in range(3)]
            vacc[rk, 0:128] += nn(low[0], g_views[0]) + nn(low[1], g_views[1])
            vacc[rk, 128:192] += nn(low[2], g_views[2])
            kacc[rk, 0:128] += nn(dss[0], q_views[0]) + nn(dss[1], q_views[1])
            kacc[rk, 128:192] += nn(dss[2], q_views[2])
            dq_pair = dq_pair + tn(dss[0], k_pair * masks[0]) + tn(dss[1], k_pair * masks[1])
            dq_last = dq_last + tn(dss[2], k_last)
            return dq_pair, dq_last

        low_tile = meta[4 + i]
        carry = (jnp.zeros((TILE, 128), f32), jnp.zeros((TILE, HEAD), f32))
        carry = lax.fori_loop(
            low_tile, own_tiles, lambda jt, cc: tile_step(jt, 0, kh, vh, kha, vha, cc), carry
        )
        carry = lax.fori_loop(
            jnp.maximum(low_tile, own_tiles),
            own_tiles + i + 1,
            lambda jt, cc: tile_step(jt, own_tiles, k, v, ka, va, cc),
            carry,
        )
        dq[r, 0:128] = (carry[0] * 0.125).astype(bf16)
        dq[r, 128:192] = (carry[1] * 0.125).astype(bf16)
        return 0

    lax.fori_loop(0, own_tiles, q_block, 0)
    dk[...] = ka[...].astype(bf16)
    dv[...] = va[...].astype(bf16)
    dkh[...] = kha[...].astype(bf16)
    dvh[...] = vha[...].astype(bf16)
    qvsum[0:1, :] = jnp.sum(dq[...].astype(f32), axis=0, keepdims=True)
    qvsum[1:2, :] = jnp.sum(dv[...].astype(f32), axis=0, keepdims=True) + jnp.sum(
        dvh[...].astype(f32), axis=0, keepdims=True
    )


def attend_back(meta, doc, q, k, v, kh, vh, ot, lse, ds_in, parts):
    total, width = q.shape
    dim = ds_in[0].shape[1]
    outs = [((total, width), bf16)] * 5 + [((total, dim), bf16), ((2, width), f32)]
    return call(
        partial(attend_back_body, len(parts)),
        outs,
        [SM] + [VM] * 8 + [ANY] * (4 + len(parts)),
        [pltpu.VMEM((width, dim), bf16)]
        + [pltpu.VMEM((total, width), f32)] * 4
        + [pltpu.SemaphoreType.DMA((6,))],
        "attend_back",
    )(meta, doc, q, k, v, kh, vh, ot, lse, *ds_in, *parts)


def attn_grads_kernel(split, meta, dq, dk, dv, dkh, dvh, n1, n1h, ot, dhb, *outs):
    picks = halves(meta[1], split, n1.shape[1])
    n = len(picks)
    width = dq.shape[1]
    for pick, wout, out in list(zip(picks, outs[:n], outs[n:]))[::-1]:
        own, far = n1[:, pick], n1h[:, pick]
        wout[0:width, :] = tn(dq[...], own).astype(bf16)
        wout[width : 2 * width, :] = (tn(dk[...], own) + tn(dkh[...], far)).astype(bf16)
        wout[2 * width :, :] = (tn(dv[...], own) + tn(dvh[...], far)).astype(bf16)
        out[...] = nn(ot[...], dhb[:, pick]).astype(bf16)


def attn_grads(meta, dq, dk, dv, dkh, dvh, n1, n1h, ot, dhb, split):
    width, dim = dq.shape[1], n1.shape[1]
    n = 2 if split else 1
    outs = [((3 * width, dim // n), bf16)] * n + [((width, dim // n), bf16)] * n
    return call(partial(attn_grads_kernel, split), outs, [SM] + [VM] * 9, [], "attn_grads")(
        meta, dq, dk, dv, dkh, dvh, n1, n1h, ot, dhb
    )


def input_grads_kernel(n_parts, *refs):
    meta, dq, dk, dv, dkh, dvh, unit, unith = refs[:8]
    parts = refs[8 : 8 + n_parts]
    outs = refs[8 + n_parts : 16 + n_parts]
    sums, wbuf, sems = refs[16 + n_parts :]
    tp, side = meta[0], meta[1]
    for one in copies(weight_pairs(parts, wbuf, side), sems):
        one.wait()
    width = dq.shape[1]
    rows = outs[0].shape[0]
    gain_sum = jnp.zeros((1, outs[0].shape[1]), f32)
    bias_sum = jnp.zeros((1, outs[0].shape[1]), f32)
    wq, wk, wv = wbuf[0:width, :], wbuf[width : 2 * width, :], wbuf[2 * width :, :]
    for j in (3, 1, 2, 0):
        r = pl.ds(rows_of(tp, j, rows), rows)
        far = nn(dkh[r, :], wk) + nn(dvh[r, :], wv)
        outs[4 + j][...] = far.astype(bf16)
        gain_sum += jnp.sum(far * unith[r, :].astype(f32), axis=0, keepdims=True)
        bias_sum += jnp.sum(far, axis=0, keepdims=True)
    for j in (3, 1, 2, 0):
        r = pl.ds(rows_of(tp, j, rows), rows)
        own = nn(dq[r, :], wq) + nn(dk[r, :], wk) + nn(dv[r, :], wv)
        outs[j][...] = own.astype(bf16)
        gain_sum += jnp.sum(own * unit[r, :].astype(f32), axis=0, keepdims=True)
        bias_sum += jnp.sum(own, axis=0, keepdims=True)
    sums[...] = jnp.zeros_like(sums)
    sums[0:1, :] = gain_sum
    sums[1:2, :] = bias_sum


def input_grads(meta, dq, dk, dv, dkh, dvh, unit, unith, parts):
    total, dim = unit.shape
    width = dq.shape[1]
    outs = [((total // 4, dim), bf16)] * 8 + [((8, dim), f32)]
    return call(
        partial(input_grads_kernel, len(parts)),
        outs,
        [SM] + [VM] * 7 + [ANY] * len(parts),
        [pltpu.VMEM((3 * width, dim), bf16), pltpu.SemaphoreType.DMA((2,))],
        "input_grads",
    )(meta, dq, dk, dv, dkh, dvh, unit, unith, *parts)


def back_one_body(x, dh, d0, dc, dx, dz, gains, out):
    dn = (
        d0[...].astype(f32) + dc[...].astype(f32) + dx[...].astype(f32) + dz[...].astype(f32)
    )
    gain = gains[0:1, :].astype(f32)
    _, unit, inverse = norm_rows(x[...].astype(f32), gain, 0.0)
    out[...] = (dh[...] + norm_back(dn, unit, inverse, gain)).astype(bf16)


def back_one(x, dh, d0, dc, dx, dz, gains):
    rows, dim = x.shape
    return call(back_one_body, [((rows, dim), bf16)], [VM] * 7, [], "back_one")(
        x, dh, d0, dc, dx, dz, gains
    )[0]


def flip(value, axis, bit):
    size = lax.axis_size(axis)
    return lax.ppermute(value, axis, [(i, i ^ bit) for i in range(size)])


def after(value, *others):
    return lax.optimization_barrier((value,) + others)[0]


def gather_four(own):
    near = flip(own, "tp", 1)
    far = flip(own, "tp", 2)
    return [own, near, far, flip(far, "tp", 1)]


def add_low(a, b):
    return (a.astype(f32) + b.astype(f32)).astype(bf16)


def scatter_four(p0, p1, p2, p3):
    far = flip(add_low(p2, flip(p3, "tp", 1)), "tp", 2)
    return p0, flip(p1, "tp", 1), far


def sum_ctx(value):
    size = lax.axis_size("ctx")
    if size != 4:
        return lax.psum(value, "ctx").astype(f32)
    place = lax.axis_index("ctx")
    first = add_low(value, lax.ppermute(value, "ctx", [(0, 1), (3, 2)]))
    second = add_low(first, lax.ppermute(first, "ctx", [(1, 2), (2, 1)]))
    third = lax.ppermute(second, "ctx", [(1, 0), (2, 3)])
    inner = (place == 1) | (place == 2)
    return jnp.where(inner, second, third).astype(f32)


def sum_shards(pieces):
    if len(pieces) == 1:
        mine = lax.psum_scatter(pieces[0], "fsdp", scatter_dimension=1, tiled=True)
    else:
        mine = add_low(pieces[0], flip(pieces[1], "fsdp", 1))
    return sum_ctx(mine)


def per_device(
    hidden,
    latent,
    latent_mask,
    segment_ids,
    norm_gains,
    row_biases,
    qv_bias,
    fc_bias,
    w_qkv,
    w_out,
    w_fc,
    w_proj,
    cotangent,
):
    own_rows, dim = hidden.shape
    part_width = w_qkv.shape[1]
    hidden_here = w_fc.shape[0]
    row_count = 4 * own_rows
    split = lax.axis_size("fsdp") == 2
    tp, side, place = lax.axis_index("tp"), lax.axis_index("fsdp"), lax.axis_index("ctx")

    x = jnp.where((latent_mask == 1)[:, None], latent, hidden)
    x_prev = lax.ppermute(x, "ctx", [(i, i + 1) for i in range(lax.axis_size("ctx") - 1)])
    xs = gather_four(x)

    def gathered(value, *late):
        value = after(value, *late)
        if split:
            return [value, flip(value, "fsdp", 1)]
        return [lax.all_gather(value, "fsdp", axis=1, tiled=True)]

    w_rows = w_qkv.reshape(3 * part_width, w_qkv.shape[2])
    qkv_parts = gathered(w_rows)

    ids = segment_ids[0]
    first_pos = place * row_count
    own_ids = lax.dynamic_slice_in_dim(ids, first_pos, row_count)
    docs = jnp.arange(32, dtype=jnp.int32)
    starts = jnp.sum((ids[None, :] < docs[:, None]).astype(jnp.int32), axis=1)
    doc_row = jnp.sum(
        jnp.where(own_ids[None, :] == docs[:, None], starts[:, None], 0), axis=0
    ) - (first_pos - row_count)
    doc = doc_row[None, :]
    lows = jnp.maximum(doc_row[::TILE], 0) // TILE
    meta = jnp.concatenate(
        [jnp.stack([tp, side, place, place]).astype(jnp.int32), lows.astype(jnp.int32)]
    )

    n1, unit, q, k, v, vt = project(
        False, meta, norm_gains, row_biases, qv_bias, xs, qkv_parts
    )
    xhs = gather_four(after(x_prev, xs[2]))
    out_parts = gathered(w_out, qkv_parts[-1])
    n1h, unith, kh, vh, vth = project(
        True, meta, norm_gains, row_biases, qv_bias, xhs, qkv_parts
    )
    dys = gather_four(after(cotangent, xhs[2]))
    fc_parts = gathered(w_fc, out_parts[-1])
    proj_parts = gathered(w_proj, fc_parts[-1])
    a0, a1, a2, a3, ot, lse = attend(
        meta, doc, q, k, v, vt, kh, vh, vth, out_parts, dim
    )
    h, n2 = residual(x, *scatter_four(a0, a1, a2, a3), norm_gains, row_biases)
    n2s = gather_four(n2)
    fcb = fc_bias[None, :]
    d0, d1, d2, d3, act, du, n2_all, dy_all, fc_sum = ffn(
        meta, fcb, n2s, dys, fc_parts, proj_parts
    )
    dn2 = scatter_four(d0, d1, d2, d3)
    gp = ffn_grads(meta, act, du, n2_all, dy_all, split)
    y0, y1, y2, y3 = ffn_out(meta, act, proj_parts)
    dh, dhb, sums_two = back_two(h, cotangent, *dn2, norm_gains)
    dhs = gather_four(dhb)
    y0, y1, y2 = scatter_four(*[after(y, dhs[2]) for y in (y0, y1, y2, y3)])
    block_out = (
        h + (y0.astype(f32) + y1.astype(f32) + y2.astype(f32)) + row_biases[3].astype(f32)
    ).astype(bf16)
    n = len(gp) // 2
    shard_proj = sum_shards(gp[:n])
    shard_fc = sum_shards(gp[n:])

    dq, dk, dv, dkh, dvh, dhb_all, qv_sum = attend_back(
        meta, doc, q, k, v, kh, vh, ot, lse, dhs, out_parts
    )
    ga = attn_grads(meta, dq, dk, dv, dkh, dvh, n1, n1h, ot, dhb_all, split)
    n = len(ga) // 2
    shard_qkv = sum_shards(ga[:n])
    shard_out = sum_shards(ga[n:])
    *dn1, sums_one = input_grads(meta, dq, dk, dv, dkh, dvh, unit, unith, qkv_parts)
    hz0, hz1, hz2 = scatter_four(*dn1[4:])
    far = add_low(hz0.astype(f32) + hz1.astype(f32), hz2)
    back = lax.ppermute(far, "ctx", [(i + 1, i) for i in range(lax.axis_size("ctx") - 1)])
    own = scatter_four(*dn1[:4])
    grad_input = back_one(x, dh, *own, back, norm_gains)

    small = jnp.concatenate([sums_two[0:4], sums_one[0:2]], axis=0)
    small = small + flip(small, "tp", 1)
    small = small + flip(small, "tp", 2)
    column = tp * part_width
    small = lax.dynamic_slice_in_dim(small, column, part_width, 1)
    small = jnp.concatenate([small, qv_sum, fc_sum.reshape(-1, part_width)], axis=0)
    if split:
        small = small + flip(small, "fsdp", 1)
    else:
        small = lax.psum(small, "fsdp")
    if lax.axis_size("ctx") == 4:
        small = small + flip(small, "ctx", 1)
        small = small + flip(small, "ctx", 2)
    else:
        small = lax.psum(small, "ctx")
    grad_gains = jnp.stack([small[4], small[0]])
    grad_biases = jnp.stack([small[5], small[1], small[2], small[3]])
    grad_qv = small[6:8]
    grad_fcb = small[8:].reshape(-1)
    return (
        block_out,
        grad_input,
        shard_qkv.reshape(3, part_width, -1),
        shard_out,
        shard_fc,
        shard_proj,
        grad_gains,
        grad_biases,
        grad_qv,
        grad_fcb,
    )


def solution(mesh):
    placed = (
        P(("fsdp", "ctx", "tp"), None),
        P(("fsdp", "ctx", "tp"), None),
        P(("fsdp", "ctx", "tp")),
        P("fsdp", None),
        P(),
        P(),
        P(None, "tp"),
        P("tp"),
        P(None, "tp", "fsdp"),
        P("tp", "fsdp"),
        P("tp", "fsdp"),
        P("tp", "fsdp"),
        P(("fsdp", "ctx", "tp"), None),
    )
    return jax.shard_map(
        per_device,
        mesh=mesh,
        in_specs=placed,
        out_specs=(
            P(("fsdp", "ctx", "tp"), None),
            P(("fsdp", "ctx", "tp"), None),
            P(None, "tp", "fsdp"),
            P("tp", "fsdp"),
            P("tp", "fsdp"),
            P("tp", "fsdp"),
            P(None, "tp"),
            P(None, "tp"),
            P(None, "tp"),
            P("tp"),
        ),
        check_vma=False,
    )
```

```python
from functools import partial

import jax
import jax.numpy as jnp
from jax import lax
from jax.experimental import pallas as pl
from jax.experimental.pallas import tpu as pltpu
from jax.sharding import PartitionSpec as P

HEAD = 64
TILE = 256
epsilon = 1e-05
masked_score = -1e30
f32 = jnp.float32
bf16 = jnp.bfloat16

VM = pl.BlockSpec(memory_space=pltpu.VMEM)
SM = pl.BlockSpec(memory_space=pltpu.SMEM)


def nn(a, b):
    return lax.dot_general(a, b, (((1,), (0,)), ((), ())), preferred_element_type=f32)


def nt(a, b):
    return lax.dot_general(a, b, (((1,), (1,)), ((), ())), preferred_element_type=f32)


def tn(a, b):
    return lax.dot_general(a, b, (((0,), (0,)), ((), ())), preferred_element_type=f32)


def call(body, outs, specs, scratch, name, us):
    return pl.pallas_call(
        body,
        out_shape=[jax.ShapeDtypeStruct(s, d) for s, d in outs],
        in_specs=specs,
        out_specs=[VM] * len(outs),
        scratch_shapes=scratch,
        name=name,
        compiler_params=pltpu.CompilerParams(vmem_limit_bytes=16 << 20),
        cost_estimate=pl.CostEstimate(
            flops=0, transcendentals=0, bytes_accessed=int(us * 3.0e4)
        ),
    )


def whole_weight(parts, dst, side):
    if len(parts) == 1:
        return parts[0]
    width = parts[0].shape[1]
    dst[:, pl.ds(pl.multiple_of(side * width, 128), width)] = parts[0][...]
    dst[:, pl.ds(pl.multiple_of((1 - side) * width, 128), width)] = parts[1][...]
    return dst


def norm_rows(values, gain, shift):
    mean = jnp.mean(values, axis=-1, keepdims=True)
    centered = values - mean
    variance = jnp.mean(centered * centered, axis=-1, keepdims=True)
    inverse = lax.rsqrt(variance + epsilon)
    unit = centered * inverse
    return unit * gain + shift, unit, inverse


def rows_of(tp, j, rows):
    return pl.multiple_of(lax.bitwise_xor(tp, j) * rows, rows)


def pick_kernel(mask, latent, hidden, out):
    for i in range(mask.shape[0]):
        column = jnp.transpose(jnp.broadcast_to(mask[i : i + 1, :], (128, 128)))[:, 0:1]
        r = slice(i * 128, (i + 1) * 128)
        chosen = jnp.where(column == 1, latent[r, :].astype(f32), hidden[r, :].astype(f32))
        out[r, :] = chosen.astype(bf16)


def pick(mask, latent, hidden):
    return call(pick_kernel, [(hidden.shape, bf16)], [VM] * 3, [], "pick", 0.5)(
        mask.reshape(-1, 128), latent, hidden
    )[0]


def project_body(n_parts, halo, *refs):
    meta, gains, biases, qvb = refs[:4]
    xs = refs[4:8]
    parts = refs[8 : 8 + n_parts]
    outs = refs[8 + n_parts :]
    if halo:
        n1, unit, k, v, vt, wbuf = outs
    else:
        n1, unit, q, k, v, vt, wbuf = outs
    width = k.shape[1]
    rows = xs[0].shape[0]
    tp, side = meta[0], meta[1]
    wbuf = whole_weight(parts, wbuf, side)
    gain = gains[0:1, :].astype(f32)
    shift = biases[0:1, :].astype(f32)
    bias_q = qvb[0:1, :].astype(f32)
    bias_v = qvb[1:2, :].astype(f32)
    bias_vt = jnp.transpose(jnp.broadcast_to(bias_v, (128, width)))[:, 0:1]
    for j in range(4):
        normed, unit_rows, _ = norm_rows(xs[j][...].astype(f32), gain, shift)
        low = normed.astype(bf16)
        r = pl.ds(rows_of(tp, j, rows), rows)
        n1[r, :] = low
        unit[r, :] = unit_rows.astype(bf16)
        if not halo:
            q[r, :] = ((nt(low, wbuf[0:width, :]) + bias_q).astype(bf16) * 0.125).astype(bf16)
        k[r, :] = nt(low, wbuf[width : 2 * width, :]).astype(bf16)
        v[r, :] = (nt(low, wbuf[2 * width :, :]) + bias_v).astype(bf16)
        vt[:, r] = (nt(wbuf[2 * width :, :], low) + bias_vt).astype(bf16)


def project(halo, meta, gains, biases, qvb, xs, parts):
    rows, dim = xs[0].shape
    width = parts[0].shape[0] // 3
    total = 4 * rows
    outs = [((total, dim), bf16), ((total, dim), bf16)]
    if not halo:
        outs.append(((total, width), bf16))
    outs += [((total, width), bf16), ((total, width), bf16), ((width, total), bf16)]
    return call(
        partial(project_body, len(parts), halo),
        outs,
        [SM, VM, VM, VM] + [VM] * (4 + len(parts)),
        [pltpu.VMEM((3 * width, dim), bf16)],
        "project_halo" if halo else "project_own",
        5,
    )(meta, gains, biases, qvb, *xs, *parts)


def lane_masks():
    lane = lax.broadcasted_iota(jnp.int32, (1, 128), 1)
    low = jnp.where(lane < HEAD, 1.0, 0.0).astype(bf16)
    return low, (1.0 - low.astype(f32)).astype(bf16)


def head_views(block, masks):
    pair = block[:, 0:128]
    return (pair * masks[0], pair * masks[1], block[:, 128:192])


def scores_of(k_pair, k_last, q_views, allowed):
    sides = (nt(k_pair, q_views[0]), nt(k_pair, q_views[1]), nt(k_last, q_views[2]))
    return [jnp.where(allowed, one, masked_score) for one in sides]


def allowed_in(jt, i, doc_row, own_tiles):
    key = jt * TILE + lax.broadcasted_iota(jnp.int32, (TILE, TILE), 0)
    query = (own_tiles + i) * TILE + lax.broadcasted_iota(jnp.int32, (1, TILE), 1)
    return (key >= doc_row) & (key <= query)


def attend_body(n_parts, *refs):
    meta, doc, q, k, v, vt, kh, vh, vth = refs[:9]
    parts = refs[9 : 9 + n_parts]
    a0, a1, a2, a3, ot, lse, wbuf = refs[9 + n_parts :]
    tp, side = meta[0], meta[1]
    total, width = q.shape
    own_tiles = total // TILE
    wbuf = whole_weight(parts, wbuf, side)
    masks = lane_masks()

    def q_block(i, _):
        r = pl.ds(pl.multiple_of(i * TILE, TILE), TILE)
        q_views = head_views(q[r, :], masks)
        doc_row = doc[0:1, r]
        start = (
            tuple(jnp.full((1, TILE), masked_score, f32) for _ in range(3)),
            tuple(jnp.zeros((1, TILE), f32) for _ in range(3)),
            tuple(jnp.zeros((HEAD, TILE), f32) for _ in range(3)),
        )

        def tile_step(jt, base, kk, vv, carry):
            rk = pl.ds(pl.multiple_of((jt - base) * TILE, TILE), TILE)
            highs, sums, accs = carry
            sides = scores_of(
                kk[rk, 0:128], kk[rk, 128:192], q_views, allowed_in(jt, i, doc_row, own_tiles)
            )
            new_h, new_s, new_a = [], [], []
            for h in range(3):
                high = jnp.maximum(highs[h], jnp.max(sides[h], axis=0, keepdims=True))
                shrink = jnp.exp(highs[h] - high)
                p = jnp.exp(sides[h] - high)
                new_h.append(high)
                new_s.append(sums[h] * shrink + jnp.sum(p, axis=0, keepdims=True))
                vv_h = vv[h * HEAD : (h + 1) * HEAD, rk]
                new_a.append(accs[h] * shrink + nn(vv_h, p.astype(bf16)))
            return tuple(new_h), tuple(new_s), tuple(new_a)

        low = meta[4 + i]
        carry = lax.fori_loop(
            low, own_tiles, lambda jt, cc: tile_step(jt, 0, kh, vth, cc), start
        )
        carry = lax.fori_loop(
            jnp.maximum(low, own_tiles),
            own_tiles + i + 1,
            lambda jt, cc: tile_step(jt, own_tiles, k, vt, cc),
            carry,
        )
        highs, sums, accs = carry
        for h in range(3):
            ot[h * HEAD : (h + 1) * HEAD, r] = (accs[h] / sums[h]).astype(bf16)
            lse[h : h + 1, r] = highs[h] + jnp.log(sums[h])
        return 0

    lax.fori_loop(0, own_tiles, q_block, 0)
    rows = a0.shape[0]
    for j, out in ((3, a3), (1, a1), (2, a2), (0, a0)):
        r = pl.ds(rows_of(tp, j, rows), rows)
        out[...] = tn(ot[:, r], wbuf[...]).astype(bf16)


def attend(meta, doc, q, k, v, vt, kh, vh, vth, parts, dim):
    total, width = q.shape
    rows = total // 4
    outs = [((rows, dim), bf16)] * 4 + [((width, total), bf16), ((8, total), f32)]
    return call(
        partial(attend_body, len(parts)),
        outs,
        [SM] + [VM] * 8 + [VM] * len(parts),
        [pltpu.VMEM((width, dim), bf16)],
        "attend",
        7,
    )(meta, doc, q, k, v, vt, kh, vh, vth, *parts)


def resid_body(x, a0, ac, ax, gains, biases, h_out, n2_out):
    h = (
        x[...].astype(f32)
        + (a0[...].astype(f32) + ac[...].astype(f32) + ax[...].astype(f32))
        + biases[2:3, :].astype(f32)
    )
    h_out[...] = h
    normed, _, _ = norm_rows(
        h.astype(bf16).astype(f32), gains[1:2, :].astype(f32), biases[1:2, :].astype(f32)
    )
    n2_out[...] = normed.astype(bf16)


def residual(x, a0, ac, ax, gains, biases):
    rows, dim = x.shape
    return call(
        resid_body, [((rows, dim), f32), ((rows, dim), bf16)], [VM] * 6, [], "residual", 1.5
    )(x, a0, ac, ax, gains, biases)


def ffn_kernel(n_parts, *refs):
    meta, fcb = refs[:2]
    n2s = refs[2:6]
    dys = refs[6:10]
    fcs = refs[10 : 10 + n_parts]
    projs = refs[10 + n_parts : 10 + 2 * n_parts]
    d0, d1, d2, d3, act, du, fcsum, fcw, pjw = refs[10 + 2 * n_parts :]
    side = meta[1]
    rows = n2s[0].shape[0]
    fcw = whole_weight(fcs, fcw, side)
    pjw = whole_weight(projs, pjw, side)
    bias = fcb[...].astype(f32)
    outs = (d0, d1, d2, d3)
    sums = jnp.zeros((1, fcw.shape[0]), f32)
    c0 = 0.7978845608028654
    c1 = 0.044715
    for j in range(4):
        r = pl.ds(j * rows, rows)
        u = nt(n2s[j][...], fcw[...]) + bias
        sq = u * u
        th = jnp.tanh(c0 * u * (1.0 + c1 * sq))
        half = 0.5 * (1.0 + th)
        act[r, :] = (u * half).astype(bf16)
        slope = half + (0.5 * c0) * u * (1.0 - th * th) * (1.0 + (3.0 * c1) * sq)
        grad = (nt(dys[j][...], pjw[...]) * slope).astype(bf16)
        du[r, :] = grad
        sums = sums + jnp.sum(grad.astype(f32), axis=0, keepdims=True)
        outs[j][...] = nn(grad, fcw[...]).astype(bf16)
    fcsum[...] = sums


def ffn(meta, fcb, n2s, dys, fcs, projs):
    rows, dim = n2s[0].shape
    hidden = fcs[0].shape[0]
    total = 4 * rows
    outs = [((rows, dim), bf16)] * 4
    outs += [((total, hidden), bf16)] * 2 + [((1, hidden), f32)]
    return call(
        partial(ffn_kernel, len(fcs)),
        outs,
        [SM, VM] + [VM] * (8 + 2 * len(fcs)),
        [pltpu.VMEM((hidden, dim), bf16), pltpu.VMEM((hidden, dim), bf16)],
        "ffn",
        8,
    )(meta, fcb, *n2s, *dys, *fcs, *projs)


def halves(side, split, width):
    if not split:
        return [pl.ds(0, width)]
    part = width // 2
    return [
        pl.ds(pl.multiple_of(side * part, 128), part),
        pl.ds(pl.multiple_of((1 - side) * part, 128), part),
    ]


def ffn_grads_kernel(split, meta, act, du, *refs):
    n2s, dys = refs[:4], refs[4:8]
    *outs, n2, dy = refs[8:]
    side = meta[1]
    picks = halves(side, split, n2.shape[1])
    n = len(picks)
    rows = n2s[0].shape[0]
    for j in range(4):
        dy[pl.ds(j * rows, rows), :] = dys[j][...]
        n2[pl.ds(j * rows, rows), :] = n2s[j][...]
    for pick, out in zip(picks[::-1], outs[:n][::-1]):
        out[...] = tn(act[...], dy[:, pick]).astype(bf16)
    for pick, out in zip(picks[::-1], outs[n:][::-1]):
        out[...] = tn(du[...], n2[:, pick]).astype(bf16)


def ffn_grads(meta, act, du, n2s, dys, split):
    total, hidden = act.shape
    dim = n2s[0].shape[1]
    n = 2 if split else 1
    outs = [((hidden, dim // n), bf16)] * (2 * n)
    return call(
        partial(ffn_grads_kernel, split),
        outs,
        [SM] + [VM] * 10,
        [pltpu.VMEM((total, dim), bf16)] * 2,
        "ffn_grads",
        6,
    )(meta, act, du, *n2s, *dys)


def ffn_out_kernel(n_parts, *refs):
    meta, act = refs[:2]
    parts = refs[2 : 2 + n_parts]
    outs = refs[2 + n_parts : 6 + n_parts]
    pjw = whole_weight(parts, refs[6 + n_parts], meta[1])
    rows = outs[0].shape[0]
    for j in range(4):
        outs[j][...] = nn(act[pl.ds(j * rows, rows), :], pjw[...]).astype(bf16)


def ffn_out(meta, act, parts):
    total, hidden = act.shape
    dim = parts[0].shape[1] * len(parts)
    return call(
        partial(ffn_out_kernel, len(parts)),
        [((total // 4, dim), bf16)] * 4,
        [SM, VM] + [VM] * len(parts),
        [pltpu.VMEM((hidden, dim), bf16)],
        "ffn_out",
        3,
    )(meta, act, *parts)


def norm_back(grad, unit, inverse, gain):
    g = grad * gain
    first = jnp.mean(g, axis=-1, keepdims=True)
    second = jnp.mean(g * unit, axis=-1, keepdims=True)
    return inverse * (g - first - unit * second)


def back_two_body(h, dy, d0, dc, dx, gains, dh_out, dhb_out, sums):
    dn = d0[...].astype(f32) + dc[...].astype(f32) + dx[...].astype(f32)
    gain = gains[1:2, :].astype(f32)
    _, unit, inverse = norm_rows(h[...].astype(bf16).astype(f32), gain, 0.0)
    grad = dy[...].astype(f32)
    dh = grad + norm_back(dn, unit, inverse, gain)
    dh_out[...] = dh
    dhb_out[...] = dh.astype(bf16)
    sums[...] = jnp.zeros_like(sums)
    sums[0:1, :] = jnp.sum(dn * unit, axis=0, keepdims=True)
    sums[1:2, :] = jnp.sum(dn, axis=0, keepdims=True)
    sums[2:3, :] = jnp.sum(dh, axis=0, keepdims=True)
    sums[3:4, :] = jnp.sum(grad, axis=0, keepdims=True)


def back_two(h, dy, d0, dc, dx, gains):
    rows, dim = h.shape
    outs = [((rows, dim), f32), ((rows, dim), bf16), ((8, dim), f32)]
    return call(back_two_body, outs, [VM] * 6, [], "back_two", 1.5)(h, dy, d0, dc, dx, gains)


def attend_back_body(n_parts, *refs):
    meta, doc, q, k, v, kh, vh, ot, lse = refs[:9]
    ds_in = refs[9:13]
    parts = refs[13 : 13 + n_parts]
    dq, dk, dv, dkh, dvh, qvsum, *gouts = refs[13 + n_parts : 19 + n_parts + n_parts]
    dhb, wbuf, ka, va, kha, vha = refs[19 + 2 * n_parts :]
    tp, side = meta[0], meta[1]
    total, width = q.shape
    rows = ds_in[0].shape[0]
    own_tiles = total // TILE
    wbuf = whole_weight(parts, wbuf, side)
    for j in range(4):
        dhb[pl.ds(rows_of(tp, j, rows), rows), :] = ds_in[j][...]
    picks = halves(side, n_parts == 2, dhb.shape[1])
    for pick, out in list(zip(picks, gouts))[::-1]:
        out[...] = nn(ot[...], dhb[:, pick]).astype(bf16)
    masks = lane_masks()
    for acc in (ka, va, kha, vha):
        acc[...] = jnp.zeros_like(acc)

    def q_block(i, _):
        r = pl.ds(pl.multiple_of(i * TILE, TILE), TILE)
        q_views = head_views(q[r, :], masks)
        doc_row = doc[0:1, r]
        grad = nt(dhb[r, :], wbuf[...]).astype(bf16)
        grad_t = nt(wbuf[...], dhb[r, :]).astype(bf16).astype(f32)
        inner = ot[:, r].astype(f32) * grad_t
        deltas = [
            jnp.sum(inner[h * HEAD : (h + 1) * HEAD, :], axis=0, keepdims=True) for h in range(3)
        ]
        logs = [lse[h : h + 1, r] for h in range(3)]
        g_views = head_views(grad, masks)

        def tile_step(jt, base, kk, vv, kacc, vacc, carry):
            rk = pl.ds(pl.multiple_of((jt - base) * TILE, TILE), TILE)
            dq_pair, dq_last = carry
            k_pair, k_last = kk[rk, 0:128], kk[rk, 128:192]
            v_pair, v_last = vv[rk, 0:128], vv[rk, 128:192]
            sides = scores_of(k_pair, k_last, q_views, allowed_in(jt, i, doc_row, own_tiles))
            grads = (nt(v_pair, g_views[0]), nt(v_pair, g_views[1]), nt(v_last, g_views[2]))
            ps = [jnp.exp(sides[h] - logs[h]) for h in range(3)]
            low = [p.astype(bf16) for p in ps]
            dss = [(ps[h] * (grads[h] - deltas[h])).astype(bf16) for h in range(3)]
            vacc[rk, 0:128] += nn(low[0], g_views[0]) + nn(low[1], g_views[1])
            vacc[rk, 128:192] += nn(low[2], g_views[2])
            kacc[rk, 0:128] += nn(dss[0], q_views[0]) + nn(dss[1], q_views[1])
            kacc[rk, 128:192] += nn(dss[2], q_views[2])
            dq_pair = dq_pair + tn(dss[0], k_pair * masks[0]) + tn(dss[1], k_pair * masks[1])
            dq_last = dq_last + tn(dss[2], k_last)
            return dq_pair, dq_last

        low_tile = meta[4 + i]
        carry = (jnp.zeros((TILE, 128), f32), jnp.zeros((TILE, HEAD), f32))
        carry = lax.fori_loop(
            low_tile, own_tiles, lambda jt, cc: tile_step(jt, 0, kh, vh, kha, vha, cc), carry
        )
        carry = lax.fori_loop(
            jnp.maximum(low_tile, own_tiles),
            own_tiles + i + 1,
            lambda jt, cc: tile_step(jt, own_tiles, k, v, ka, va, cc),
            carry,
        )
        dq[r, 0:128] = (carry[0] * 0.125).astype(bf16)
        dq[r, 128:192] = (carry[1] * 0.125).astype(bf16)
        return 0

    lax.fori_loop(0, own_tiles, q_block, 0)
    dk[...] = ka[...].astype(bf16)
    dv[...] = va[...].astype(bf16)
    dkh[...] = kha[...].astype(bf16)
    dvh[...] = vha[...].astype(bf16)
    qvsum[0:1, :] = jnp.sum(dq[...].astype(f32), axis=0, keepdims=True)
    qvsum[1:2, :] = jnp.sum(dv[...].astype(f32), axis=0, keepdims=True) + jnp.sum(
        dvh[...].astype(f32), axis=0, keepdims=True
    )


def attend_back(meta, doc, q, k, v, kh, vh, ot, lse, ds_in, parts):
    total, width = q.shape
    dim = ds_in[0].shape[1]
    n = len(parts)
    outs = [((total, width), bf16)] * 5 + [((2, width), f32)] + [((width, dim // n), bf16)] * n
    return call(
        partial(attend_back_body, len(parts)),
        outs,
        [SM] + [VM] * 8 + [VM] * (4 + len(parts)),
        [pltpu.VMEM((total, dim), bf16), pltpu.VMEM((width, dim), bf16)]
        + [pltpu.VMEM((total, width), f32)] * 4,
        "attend_back",
        11,
    )(meta, doc, q, k, v, kh, vh, ot, lse, *ds_in, *parts)


def attn_grads_kernel(split, meta, dq, dk, dv, dkh, dvh, n1, n1h, *outs):
    picks = halves(meta[1], split, n1.shape[1])
    width = dq.shape[1]
    for pick, wout in list(zip(picks, outs))[::-1]:
        own, far = n1[:, pick], n1h[:, pick]
        wout[0:width, :] = tn(dq[...], own).astype(bf16)
        wout[width : 2 * width, :] = (tn(dk[...], own) + tn(dkh[...], far)).astype(bf16)
        wout[2 * width :, :] = (tn(dv[...], own) + tn(dvh[...], far)).astype(bf16)


def attn_grads(meta, dq, dk, dv, dkh, dvh, n1, n1h, split):
    width, dim = dq.shape[1], n1.shape[1]
    n = 2 if split else 1
    outs = [((3 * width, dim // n), bf16)] * n
    return call(partial(attn_grads_kernel, split), outs, [SM] + [VM] * 7, [], "attn_grads", 5)(
        meta, dq, dk, dv, dkh, dvh, n1, n1h
    )


def put_pair(ref, at, value):
    high = value.astype(bf16)
    ref[at : at + 8, :] = high
    ref[at + 8 : at + 16, :] = (value - high.astype(f32)).astype(bf16)


def take_pair(ref, at):
    value = ref[at : at + 8, :].astype(f32) + ref[at + 8 : at + 16, :].astype(f32)
    row = lax.broadcasted_iota(jnp.int32, value.shape, 0)
    return jnp.where(row < 6, value, 0.0)


def halo_mid_kernel(h2, got, sums, mid, sums_out):
    rows = h2.shape[0]
    mid[0:rows, :] = (h2[...].astype(f32) + got[0:rows, :].astype(f32)).astype(bf16)
    value = sums[...] + take_pair(got, rows)
    sums_out[...] = value
    put_pair(mid, rows, value)


def halo_mid(h2, got, sums):
    outs = [(got.shape, bf16), (sums.shape, f32)]
    return call(halo_mid_kernel, outs, [VM] * 3, [], "halo_mid", 0.5)(h2, got, sums)


def halo_end_kernel(h0, rest, got, sums, far, sums_out):
    rows = h0.shape[0]
    value = h0[...].astype(f32) + rest[0:rows, :].astype(f32) + got[0:rows, :].astype(f32)
    far[...] = value.astype(bf16)
    sums_out[...] = sums[...] + take_pair(got, rows)


def halo_end(h0, rest, got, sums):
    outs = [(h0.shape, bf16), (sums.shape, f32)]
    return call(halo_end_kernel, outs, [VM] * 4, [], "halo_end", 0.5)(h0, rest, got, sums)


def own_mid_kernel(o2, rest, out):
    rows = o2.shape[0]
    out[...] = (o2[...].astype(f32) + rest[2 * rows : 3 * rows, :].astype(f32)).astype(bf16)


def own_mid(o2, rest):
    return call(own_mid_kernel, [(o2.shape, bf16)], [VM] * 2, [], "own_mid", 0.5)(o2, rest)[0]


def round_kernel(n_add, n_pick, *refs):
    meta = refs[0]
    ins, outs = refs[1 : 1 + 2 * (n_add + n_pick)], refs[1 + 2 * (n_add + n_pick) :]
    for i in range(n_add):
        total = ins[2 * i][...].astype(f32) + ins[2 * i + 1][...].astype(f32)
        outs[i][...] = total.astype(bf16)
    inner = (meta[2] == 1) | (meta[2] == 2)
    for i in range(n_add, n_add + n_pick):

        @pl.when(inner)
        def _():
            outs[i][...] = ins[2 * i][...].astype(f32)

        @pl.when(jnp.logical_not(inner))
        def _():
            outs[i][...] = ins[2 * i + 1][...].astype(f32)


def round_of(meta, adds, picks=()):
    flat = [one for pair in (*adds, *picks) for one in pair]
    outs = [(pair[0].shape, bf16) for pair in adds] + [(pair[0].shape, f32) for pair in picks]
    return call(
        partial(round_kernel, len(adds), len(picks)),
        outs,
        [SM] + [VM] * len(flat),
        [],
        "round",
        0.5,
    )(meta, *flat)


def input_grads_kernel(n_parts, *refs):
    meta, dq, dk, dv, dkh, dvh, unit, unith, two, fcsum, qvsum = refs[:11]
    parts = refs[11 : 11 + n_parts]
    o0, o2, h0, h2, near, rest, sums, wbuf = refs[11 + n_parts :]
    tp, side = meta[0], meta[1]
    wbuf = whole_weight(parts, wbuf, side)
    width = dq.shape[1]
    rows, dim = o0.shape
    gain_sum = jnp.zeros((1, dim), f32)
    bias_sum = jnp.zeros((1, dim), f32)
    wq, wk, wv = wbuf[0:width, :], wbuf[width : 2 * width, :], wbuf[2 * width :, :]
    far_outs = {0: h0, 1: rest.at[0:rows], 2: h2, 3: near.at[0:rows]}
    own_outs = {0: o0, 1: rest.at[rows : 2 * rows], 2: o2, 3: rest.at[2 * rows : 3 * rows]}
    for j in range(4):
        r = pl.ds(rows_of(tp, j, rows), rows)
        far = nn(dkh[r, :], wk) + nn(dvh[r, :], wv)
        far_outs[j][...] = far.astype(bf16)
        gain_sum += jnp.sum(far * unith[r, :].astype(f32), axis=0, keepdims=True)
        bias_sum += jnp.sum(far, axis=0, keepdims=True)
        own = nn(dq[r, :], wq) + nn(dk[r, :], wk) + nn(dv[r, :], wv)
        own_outs[j][...] = own.astype(bf16)
        gain_sum += jnp.sum(own * unit[r, :].astype(f32), axis=0, keepdims=True)
        bias_sum += jnp.sum(own, axis=0, keepdims=True)
    sums[...] = two[...]
    sums[4:5, :] = gain_sum
    sums[5:6, :] = bias_sum
    sums[6:7, :] = fcsum[...]
    sums[7:8, 0:width] = qvsum[0:1, :]
    sums[7:8, 256 : 256 + width] = qvsum[1:2, :]
    put_pair(near, rows, sums[...])


def input_grads(meta, dq, dk, dv, dkh, dvh, unit, unith, two, fcsum, qvsum, parts):
    total, dim = unit.shape
    width = dq.shape[1]
    rows = total // 4
    outs = [((rows, dim), bf16)] * 4
    outs += [((rows + 16, dim), bf16), ((3 * rows, dim), bf16), ((8, dim), f32)]
    return call(
        partial(input_grads_kernel, len(parts)),
        outs,
        [SM] + [VM] * (10 + len(parts)),
        [pltpu.VMEM((3 * width, dim), bf16)],
        "input_grads",
        5,
    )(meta, dq, dk, dv, dkh, dvh, unit, unith, two, fcsum, qvsum, *parts)


def back_one_body(x, dh, o0, rest, far, halo, gains, out):
    rows = x.shape[0]
    dn = o0[...].astype(f32) + rest[rows : 2 * rows, :].astype(f32)
    dn = dn + far[...].astype(f32) + halo[...].astype(f32)
    gain = gains[0:1, :].astype(f32)
    _, unit, inverse = norm_rows(x[...].astype(f32), gain, 0.0)
    out[...] = (dh[...] + norm_back(dn, unit, inverse, gain)).astype(bf16)


def back_one(x, dh, o0, rest, far, halo, gains):
    rows, dim = x.shape
    return call(back_one_body, [((rows, dim), bf16)], [VM] * 7, [], "back_one", 1.5)(
        x, dh, o0, rest, far, halo, gains
    )[0]


def flip(value, axis, bit):
    size = lax.axis_size(axis)
    return lax.ppermute(value, axis, [(i, i ^ bit) for i in range(size)])


def after(value, *others):
    return lax.optimization_barrier((value,) + others)[0]


def gather_four(own):
    near = flip(own, "tp", 1)
    far = flip(own, "tp", 2)
    return [own, near, far, flip(far, "tp", 1)]


def add_low(a, b):
    return (a.astype(f32) + b.astype(f32)).astype(bf16)


def along(value, pairs):
    return lax.ppermute(value, "ctx", pairs)


def step_one(value):
    return along(value, [(0, 1), (3, 2)])


def step_two(value):
    return along(value, [(1, 2), (2, 1)])


def step_three(value):
    return along(value, [(1, 0), (2, 3)])


class Line:
    def __init__(self):
        self.last = None

    def __call__(self, step, first, *rest, also=()):
        waits = [one for one in (self.last, *also) if one is not None]
        out = step(after(first, *waits) if waits else first, *rest)
        self.last = out[0] if isinstance(out, (tuple, list)) else out
        return out


def per_device(
    hidden,
    latent,
    latent_mask,
    segment_ids,
    norm_gains,
    row_biases,
    qv_bias,
    fc_bias,
    w_qkv,
    w_out,
    w_fc,
    w_proj,
    cotangent,
):
    own_rows, dim = hidden.shape
    part_width = w_qkv.shape[1]
    hidden_here = w_fc.shape[0]
    row_count = 4 * own_rows
    split = lax.axis_size("fsdp") == 2
    tp, side, place = lax.axis_index("tp"), lax.axis_index("fsdp"), lax.axis_index("ctx")

    x = pick(latent_mask, latent, hidden)
    x_prev = lax.ppermute(x, "ctx", [(i, i + 1) for i in range(lax.axis_size("ctx") - 1)])

    def gathered(value, *late):
        value = after(value, *late)
        if split:
            return [value, flip(value, "fsdp", 1)]
        return [lax.all_gather(value, "fsdp", axis=1, tiled=True)]

    w_rows = w_qkv.reshape(3 * part_width, w_qkv.shape[2])
    qkv_parts = gathered(w_rows)
    x_far = flip(x, "tp", 2)
    xs = [x, flip(x, "tp", 1), x_far, flip(after(x_far, qkv_parts[-1]), "tp", 1)]

    ids = segment_ids[0]
    first_pos = place * row_count
    own_ids = lax.dynamic_slice_in_dim(ids, first_pos, row_count)
    docs = jnp.arange(32, dtype=jnp.int32)
    starts = jnp.sum((ids[None, :] < docs[:, None]).astype(jnp.int32), axis=1)
    doc_row = jnp.sum(
        jnp.where(own_ids[None, :] == docs[:, None], starts[:, None], 0), axis=0
    ) - (first_pos - row_count)
    doc = doc_row[None, :]
    lows = jnp.maximum(doc_row[::TILE], 0) // TILE
    meta = jnp.concatenate(
        [jnp.stack([tp, side, place, place]).astype(jnp.int32), lows.astype(jnp.int32)]
    )

    line = Line()
    n1, unit, q, k, v, vt = line(
        lambda m: project(False, m, norm_gains, row_biases, qv_bias, xs, qkv_parts), meta
    )
    xh_far = flip(after(x_prev, xs[2]), "tp", 2)
    out_parts = gathered(w_out, qkv_parts[-1])
    xhs = [
        x_prev,
        flip(x_prev, "tp", 1),
        xh_far,
        flip(after(xh_far, n1, out_parts[-1]), "tp", 1),
    ]
    fc_parts = gathered(w_fc, out_parts[-1], n1)
    proj_parts = gathered(w_proj, fc_parts[-1])
    dy_far = flip(after(cotangent, xh_far), "tp", 2)
    n1h, unith, kh, vh, vth = line(
        lambda m: project(True, m, norm_gains, row_biases, qv_bias, xhs, qkv_parts), meta
    )
    a0, a1, a2, a3, ot, lse = line(
        lambda m: attend(m, doc, q, k, v, vt, kh, vh, vth, out_parts, dim), meta
    )
    a2 = line(add_low, a2, flip(after(a3, dy_far, fc_parts[-1]), "tp", 1))
    a_far = flip(a2, "tp", 2)
    h, n2 = line(
        lambda one: residual(x, one, flip(a1, "tp", 1), a_far, norm_gains, row_biases),
        a0,
        also=(proj_parts[-1],),
    )
    dys = [cotangent, flip(cotangent, "tp", 1), dy_far, flip(dy_far, "tp", 1)]
    n2s = gather_four(n2)
    fcb = fc_bias[None, :]
    d0, d1, d2, d3, act, du, fc_sum = line(
        lambda m: ffn(m, fcb, n2s, dys, fc_parts, proj_parts), meta
    )
    d2 = line(add_low, d2, flip(d3, "tp", 1))
    d_far = flip(d2, "tp", 2)
    gp = line(lambda one: ffn_grads(meta, one, du, n2s, dys, split), act)
    y0, y1, y2, y3 = line(lambda one: ffn_out(meta, one, proj_parts), act)
    dh, dhb, sums_two = line(
        lambda one: back_two(h, cotangent, one, flip(d1, "tp", 1), d_far, norm_gains), d0
    )
    y2 = line(add_low, y2, flip(y3, "tp", 1))
    tree = lax.axis_size("ctx") == 4 and split
    if split:
        got_proj = flip(gp[1], "fsdp", 1)
        got_fc = flip(after(gp[3], got_proj), "fsdp", 1)
        mine_proj = line(add_low, gp[0], got_proj)
    else:
        mine_proj = gp[0]
    dh_far = flip(dhb, "tp", 2)
    dhs = [
        dhb,
        flip(dhb, "tp", 1),
        dh_far,
        flip(after(dh_far, mine_proj), "tp", 1),
    ]
    y_far = flip(after(y2, dh_far), "tp", 2)
    dq, dk, dv, dkh, dvh, qv_sum, *go = line(
        lambda m: attend_back(m, doc, q, k, v, kh, vh, ot, lse, dhs, out_parts), meta
    )
    if tree:
        one_proj, mine_fc = line(
            lambda m: round_of(m, [(mine_proj, step_one(mine_proj)), (gp[2], got_fc)]), meta
        )
        z_proj, z_fc = step_two(one_proj), step_one(mine_fc)
    ga = line(
        lambda one: attn_grads(meta, one, dk, dv, dkh, dvh, n1, n1h, split), dq, also=(y_far,)
    )
    if tree:
        got_qkv = flip(ga[1], "fsdp", 1)
        got_out = flip(go[1], "fsdp", 1)
    o0, o2, h0, h2, near, rest, sums = line(
        lambda one: input_grads(
            meta, one, dk, dv, dkh, dvh, unit, unith, sums_two, fc_sum, qv_sum, qkv_parts
        ),
        dq,
    )
    near = flip(near, "tp", 1)
    rest = flip(rest, "tp", 1)

    def block_end(one):
        total = one.astype(f32) + flip(y1, "tp", 1).astype(f32) + y_far.astype(f32)
        return (h + total + row_biases[3].astype(f32)).astype(bf16)

    block_out = line(block_end, y0)
    if tree:
        two_proj, one_fc, mine_qkv, mine_out = line(
            lambda m: round_of(
                m, [(one_proj, z_proj), (mine_fc, z_fc), (ga[0], got_qkv), (go[0], got_out)]
            ),
            meta,
        )
        z_proj, z_fc = step_three(two_proj), step_two(one_fc)
        z_qkv, z_out = step_one(mine_qkv), step_one(mine_out)
    mid, sums = line(halo_mid, h2, near, sums)
    mid = flip(mid, "tp", 2)
    o2 = line(own_mid, o2, rest)
    if tree:
        two_fc, one_qkv, one_out, shard_proj = line(
            lambda m: round_of(
                m, [(one_fc, z_fc), (mine_qkv, z_qkv), (mine_out, z_out)], [(two_proj, z_proj)]
            ),
            meta,
        )
        z_fc, z_qkv, z_out = step_three(two_fc), step_two(one_qkv), step_two(one_out)
    far, sums = line(halo_end, h0, rest, mid, sums)
    back = along(far, [(i + 1, i) for i in range(lax.axis_size("ctx") - 1)])
    o_far = flip(after(o2, mid), "tp", 2)
    if tree:
        got_sums = flip(sums, "fsdp", 1)
        two_qkv, two_out, shard_fc = line(
            lambda m: round_of(
                m, [(one_qkv, z_qkv), (one_out, z_out)], [(two_fc, z_fc)]
            ),
            meta,
        )
        z_qkv, z_out = step_three(two_qkv), step_three(two_out)
        sums = line(lambda one: one + got_sums, sums)
        near_sums, far_sums = flip(sums, "ctx", 1), (flip(sums, "ctx", 2), flip(sums, "ctx", 3))
        grad_input = line(
            lambda one: back_one(one, dh, o0, rest, o_far, back, norm_gains), x
        )
        sums = line(lambda one: (one + near_sums) + (far_sums[0] + far_sums[1]), sums)
        shard_qkv, shard_out = line(
            lambda m: round_of(m, [], [(two_qkv, z_qkv), (two_out, z_out)]), meta
        )
    else:
        grad_input = back_one(x, dh, o0, rest, o_far, back, norm_gains)
        sums = lax.psum(sums, ("fsdp", "ctx"))
        shard_proj, shard_fc, shard_qkv, shard_out = (
            lax.psum(
                lax.psum_scatter(one[0], "fsdp", scatter_dimension=1, tiled=True)
                if len(one) == 1
                else add_low(one[0], flip(one[1], "fsdp", 1)),
                "ctx",
            ).astype(f32)
            for one in (gp[: len(gp) // 2], gp[len(gp) // 2 :], ga, go)
        )

    small = lax.dynamic_slice_in_dim(sums[0:6], tp * part_width, part_width, 1)
    grad_gains = jnp.stack([small[4], small[0]])
    grad_biases = jnp.stack([small[5], small[1], small[2], small[3]])
    grad_qv = jnp.stack([sums[7, 0:part_width], sums[7, 256 : 256 + part_width]])
    grad_fcb = sums[6]
    return (
        block_out,
        grad_input,
        shard_qkv.reshape(3, part_width, -1),
        shard_out,
        shard_fc,
        shard_proj,
        grad_gains,
        grad_biases,
        grad_qv,
        grad_fcb,
    )


def solution(mesh):
    placed = (
        P(("fsdp", "ctx", "tp"), None),
        P(("fsdp", "ctx", "tp"), None),
        P(("fsdp", "ctx", "tp")),
        P("fsdp", None),
        P(),
        P(),
        P(None, "tp"),
        P("tp"),
        P(None, "tp", "fsdp"),
        P("tp", "fsdp"),
        P("tp", "fsdp"),
        P("tp", "fsdp"),
        P(("fsdp", "ctx", "tp"), None),
    )
    return jax.shard_map(
        per_device,
        mesh=mesh,
        in_specs=placed,
        out_specs=(
            P(("fsdp", "ctx", "tp"), None),
            P(("fsdp", "ctx", "tp"), None),
            P(None, "tp", "fsdp"),
            P("tp", "fsdp"),
            P("tp", "fsdp"),
            P("tp", "fsdp"),
            P(None, "tp"),
            P(None, "tp"),
            P(None, "tp"),
            P("tp"),
        ),
        check_vma=False,
    )
```

```python
from functools import partial

import jax
import jax.numpy as jnp
from jax import lax
from jax.experimental import pallas as pl
from jax.experimental.pallas import tpu as pltpu
from jax.sharding import PartitionSpec as P

HEAD = 64
TILE = 256
epsilon = 1e-05
masked_score = -1e30
f32 = jnp.float32
bf16 = jnp.bfloat16

VM = pl.BlockSpec(memory_space=pltpu.VMEM)
SM = pl.BlockSpec(memory_space=pltpu.SMEM)


def nn(a, b):
    return lax.dot_general(a, b, (((1,), (0,)), ((), ())), preferred_element_type=f32)


def nt(a, b):
    return lax.dot_general(a, b, (((1,), (1,)), ((), ())), preferred_element_type=f32)


def tn(a, b):
    return lax.dot_general(a, b, (((0,), (0,)), ((), ())), preferred_element_type=f32)


def call(body, outs, specs, scratch, name, us):
    return pl.pallas_call(
        body,
        out_shape=[jax.ShapeDtypeStruct(s, d) for s, d in outs],
        in_specs=specs,
        out_specs=[VM] * len(outs),
        scratch_shapes=scratch,
        name=name,
        compiler_params=pltpu.CompilerParams(vmem_limit_bytes=16 << 20),
        cost_estimate=pl.CostEstimate(
            flops=0, transcendentals=0, bytes_accessed=int(us * 3.0e4)
        ),
    )


def whole_weight(parts, dst, side):
    if len(parts) == 1:
        return parts[0]
    width = parts[0].shape[1]
    dst[:, pl.ds(pl.multiple_of(side * width, 128), width)] = parts[0][...]
    dst[:, pl.ds(pl.multiple_of((1 - side) * width, 128), width)] = parts[1][...]
    return dst


def norm_rows(values, gain, shift):
    mean = jnp.mean(values, axis=-1, keepdims=True)
    centered = values - mean
    variance = jnp.mean(centered * centered, axis=-1, keepdims=True)
    inverse = lax.rsqrt(variance + epsilon)
    unit = centered * inverse
    return unit * gain + shift, unit, inverse


def rows_of(tp, j, rows):
    return pl.multiple_of(lax.bitwise_xor(tp, j) * rows, rows)


def pick_kernel(mask, latent, hidden, out):
    for i in range(mask.shape[0]):
        column = jnp.transpose(jnp.broadcast_to(mask[i : i + 1, :], (128, 128)))[:, 0:1]
        r = slice(i * 128, (i + 1) * 128)
        chosen = jnp.where(column == 1, latent[r, :].astype(f32), hidden[r, :].astype(f32))
        out[r, :] = chosen.astype(bf16)


def pick(mask, latent, hidden):
    return call(pick_kernel, [(hidden.shape, bf16)], [VM] * 3, [], "pick", 0.5)(
        mask.reshape(-1, 128), latent, hidden
    )[0]


def project_body(n_parts, halo, *refs):
    meta, gains, biases, qvb = refs[:4]
    xs = refs[4:8]
    parts = refs[8 : 8 + n_parts]
    outs = refs[8 + n_parts :]
    if halo:
        n1, unit, k, v, vt, wbuf = outs
    else:
        n1, unit, q, k, v, vt, wbuf = outs
    width = k.shape[1]
    rows = xs[0].shape[0]
    tp, side = meta[0], meta[1]
    wbuf = whole_weight(parts, wbuf, side)
    gain = gains[0:1, :].astype(f32)
    shift = biases[0:1, :].astype(f32)
    bias_q = qvb[0:1, :].astype(f32)
    bias_v = qvb[1:2, :].astype(f32)
    bias_vt = jnp.transpose(jnp.broadcast_to(bias_v, (128, width)))[:, 0:1]
    for j in range(4):
        normed, unit_rows, _ = norm_rows(xs[j][...].astype(f32), gain, shift)
        low = normed.astype(bf16)
        r = pl.ds(rows_of(tp, j, rows), rows)
        n1[r, :] = low
        unit[r, :] = unit_rows.astype(bf16)
        if not halo:
            q[r, :] = ((nt(low, wbuf[0:width, :]) + bias_q).astype(bf16) * 0.125).astype(bf16)
        k[r, :] = nt(low, wbuf[width : 2 * width, :]).astype(bf16)
        v[r, :] = (nt(low, wbuf[2 * width :, :]) + bias_v).astype(bf16)
        vt[:, r] = (nt(wbuf[2 * width :, :], low) + bias_vt).astype(bf16)


def project(halo, meta, gains, biases, qvb, xs, parts):
    rows, dim = xs[0].shape
    width = parts[0].shape[0] // 3
    total = 4 * rows
    outs = [((total, dim), bf16), ((total, dim), bf16)]
    if not halo:
        outs.append(((total, width), bf16))
    outs += [((total, width), bf16), ((total, width), bf16), ((width, total), bf16)]
    return call(
        partial(project_body, len(parts), halo),
        outs,
        [SM, VM, VM, VM] + [VM] * (4 + len(parts)),
        [pltpu.VMEM((3 * width, dim), bf16)],
        "project_halo" if halo else "project_own",
        5,
    )(meta, gains, biases, qvb, *xs, *parts)


def lane_masks():
    lane = lax.broadcasted_iota(jnp.int32, (1, 128), 1)
    low = jnp.where(lane < HEAD, 1.0, 0.0).astype(bf16)
    return low, (1.0 - low.astype(f32)).astype(bf16)


def head_views(block, masks):
    pair = block[:, 0:128]
    return (pair * masks[0], pair * masks[1], block[:, 128:192])


def scores_of(k_pair, k_last, q_views, allowed):
    sides = (nt(k_pair, q_views[0]), nt(k_pair, q_views[1]), nt(k_last, q_views[2]))
    return [jnp.where(allowed, one, masked_score) for one in sides]


def allowed_in(jt, i, doc_row, own_tiles):
    key = jt * TILE + lax.broadcasted_iota(jnp.int32, (TILE, TILE), 0)
    query = (own_tiles + i) * TILE + lax.broadcasted_iota(jnp.int32, (1, TILE), 1)
    return (key >= doc_row) & (key <= query)


def attend_body(n_parts, *refs):
    meta, doc, q, k, v, vt, kh, vh, vth = refs[:9]
    parts = refs[9 : 9 + n_parts]
    a0, a1, a2, a3, ot, lse, wbuf = refs[9 + n_parts :]
    tp, side = meta[0], meta[1]
    total, width = q.shape
    own_tiles = total // TILE
    wbuf = whole_weight(parts, wbuf, side)
    masks = lane_masks()

    def q_block(i, _):
        r = pl.ds(pl.multiple_of(i * TILE, TILE), TILE)
        q_views = head_views(q[r, :], masks)
        doc_row = doc[0:1, r]
        start = (
            tuple(jnp.full((1, TILE), masked_score, f32) for _ in range(3)),
            tuple(jnp.zeros((1, TILE), f32) for _ in range(3)),
            tuple(jnp.zeros((HEAD, TILE), f32) for _ in range(3)),
        )

        def tile_step(jt, base, kk, vv, carry):
            rk = pl.ds(pl.multiple_of((jt - base) * TILE, TILE), TILE)
            highs, sums, accs = carry
            sides = scores_of(
                kk[rk, 0:128], kk[rk, 128:192], q_views, allowed_in(jt, i, doc_row, own_tiles)
            )
            new_h, new_s, new_a = [], [], []
            for h in range(3):
                high = jnp.maximum(highs[h], jnp.max(sides[h], axis=0, keepdims=True))
                shrink = jnp.exp(highs[h] - high)
                p = jnp.exp(sides[h] - high)
                new_h.append(high)
                new_s.append(sums[h] * shrink + jnp.sum(p, axis=0, keepdims=True))
                vv_h = vv[h * HEAD : (h + 1) * HEAD, rk]
                new_a.append(accs[h] * shrink + nn(vv_h, p.astype(bf16)))
            return tuple(new_h), tuple(new_s), tuple(new_a)

        low = meta[4 + i]
        carry = lax.fori_loop(
            low, own_tiles, lambda jt, cc: tile_step(jt, 0, kh, vth, cc), start
        )
        carry = lax.fori_loop(
            jnp.maximum(low, own_tiles),
            own_tiles + i + 1,
            lambda jt, cc: tile_step(jt, own_tiles, k, vt, cc),
            carry,
        )
        highs, sums, accs = carry
        for h in range(3):
            ot[h * HEAD : (h + 1) * HEAD, r] = (accs[h] / sums[h]).astype(bf16)
            lse[h : h + 1, r] = highs[h] + jnp.log(sums[h])
        return 0

    lax.fori_loop(0, own_tiles, q_block, 0)
    rows = a0.shape[0]
    for j, out in ((3, a3), (1, a1), (2, a2), (0, a0)):
        r = pl.ds(rows_of(tp, j, rows), rows)
        out[...] = tn(ot[:, r], wbuf[...]).astype(bf16)


def attend(meta, doc, q, k, v, vt, kh, vh, vth, parts, dim):
    total, width = q.shape
    rows = total // 4
    outs = [((rows, dim), bf16)] * 4 + [((width, total), bf16), ((8, total), f32)]
    return call(
        partial(attend_body, len(parts)),
        outs,
        [SM] + [VM] * 8 + [VM] * len(parts),
        [pltpu.VMEM((width, dim), bf16)],
        "attend",
        7,
    )(meta, doc, q, k, v, vt, kh, vh, vth, *parts)


def resid_body(x, a0, ac, ax, gains, biases, h_out, n2_out):
    h = (
        x[...].astype(f32)
        + (a0[...].astype(f32) + ac[...].astype(f32) + ax[...].astype(f32))
        + biases[2:3, :].astype(f32)
    )
    h_out[...] = h
    normed, _, _ = norm_rows(
        h.astype(bf16).astype(f32), gains[1:2, :].astype(f32), biases[1:2, :].astype(f32)
    )
    n2_out[...] = normed.astype(bf16)


def residual(x, a0, ac, ax, gains, biases):
    rows, dim = x.shape
    return call(
        resid_body, [((rows, dim), f32), ((rows, dim), bf16)], [VM] * 6, [], "residual", 1.5
    )(x, a0, ac, ax, gains, biases)


def ffn_kernel(n_parts, *refs):
    meta, fcb = refs[:2]
    n2s = refs[2:4]
    dys = refs[4:6]
    fcs = refs[6 : 6 + n_parts]
    projs = refs[6 + n_parts : 6 + 2 * n_parts]
    d0, d1, act, du, fcsum, fcw, pjw = refs[6 + 2 * n_parts :]
    side = meta[1]
    rows = n2s[0].shape[0]
    fcw = whole_weight(fcs, fcw, side)
    pjw = whole_weight(projs, pjw, side)
    bias = fcb[...].astype(f32)
    outs = (d0, d1)
    sums = jnp.zeros((1, fcw.shape[0]), f32)
    c0 = 0.7978845608028654
    c1 = 0.044715
    for j in (1, 0):
        r = pl.ds(j * rows, rows)
        u = nt(n2s[j][...], fcw[...]) + bias
        sq = u * u
        th = jnp.tanh(c0 * u * (1.0 + c1 * sq))
        half = 0.5 * (1.0 + th)
        act[r, :] = (u * half).astype(bf16)
        slope = half + (0.5 * c0) * u * (1.0 - th * th) * (1.0 + (3.0 * c1) * sq)
        grad = (nt(dys[j][...], pjw[...]) * slope).astype(bf16)
        du[r, :] = grad
        sums = sums + jnp.sum(grad.astype(f32), axis=0, keepdims=True)
        outs[j][...] = nn(grad, fcw[...]).astype(bf16)
    fcsum[...] = sums


def ffn(meta, fcb, n2s, dys, fcs, projs):
    rows, dim = n2s[0].shape
    hidden = fcs[0].shape[0]
    outs = [((rows, dim), bf16)] * 2
    outs += [((2 * rows, hidden), bf16)] * 2 + [((1, hidden), f32)]
    return call(
        partial(ffn_kernel, len(fcs)),
        outs,
        [SM, VM] + [VM] * (4 + 2 * len(fcs)),
        [pltpu.VMEM((hidden, dim), bf16), pltpu.VMEM((hidden, dim), bf16)],
        "ffn",
        4,
    )(meta, fcb, *n2s, *dys, *fcs, *projs)


def halves(side, split, width):
    if not split:
        return [pl.ds(0, width)]
    part = width // 2
    return [
        pl.ds(pl.multiple_of(side * part, 128), part),
        pl.ds(pl.multiple_of((1 - side) * part, 128), part),
    ]


def ffn_grad_kernel(split, meta, low, high, *refs):
    pieces, outs, right = refs[:4], refs[4:-1], refs[-1]
    picks = halves(meta[1], split, right.shape[1])
    rows = pieces[0].shape[0]
    for j in range(4):
        right[pl.ds(j * rows, rows), :] = pieces[j][...]
    for pick, out in zip(picks[::-1], outs[::-1]):
        total = tn(low[...], right[0 : 2 * rows, pick]) + tn(high[...], right[2 * rows :, pick])
        out[...] = total.astype(bf16)


def ffn_grad(meta, low, high, pieces, split):
    total, hidden = low.shape
    dim = pieces[0].shape[1]
    n = 2 if split else 1
    return call(
        partial(ffn_grad_kernel, split),
        [((hidden, dim // n), bf16)] * n,
        [SM] + [VM] * 6,
        [pltpu.VMEM((2 * total, dim), bf16)],
        "ffn_grad",
        3,
    )(meta, low, high, *pieces)


def ffn_out_kernel(n_parts, *refs):
    meta, low, high = refs[:3]
    parts = refs[3 : 3 + n_parts]
    outs = refs[3 + n_parts : 7 + n_parts]
    pjw = whole_weight(parts, refs[7 + n_parts], meta[1])
    rows = outs[0].shape[0]
    for j in range(4):
        act = high if j > 1 else low
        outs[j][...] = nn(act[pl.ds((j % 2) * rows, rows), :], pjw[...]).astype(bf16)


def ffn_out(meta, low, high, parts):
    total, hidden = low.shape
    dim = parts[0].shape[1] * len(parts)
    return call(
        partial(ffn_out_kernel, len(parts)),
        [((total // 2, dim), bf16)] * 4,
        [SM, VM, VM] + [VM] * len(parts),
        [pltpu.VMEM((hidden, dim), bf16)],
        "ffn_out",
        3,
    )(meta, low, high, *parts)


def norm_back(grad, unit, inverse, gain):
    g = grad * gain
    first = jnp.mean(g, axis=-1, keepdims=True)
    second = jnp.mean(g * unit, axis=-1, keepdims=True)
    return inverse * (g - first - unit * second)


def back_two_body(h, dy, d0, dc, dx, gains, dh_out, dhb_out, sums):
    dn = d0[...].astype(f32) + dc[...].astype(f32) + dx[...].astype(f32)
    gain = gains[1:2, :].astype(f32)
    _, unit, inverse = norm_rows(h[...].astype(bf16).astype(f32), gain, 0.0)
    grad = dy[...].astype(f32)
    dh = grad + norm_back(dn, unit, inverse, gain)
    dh_out[...] = dh
    dhb_out[...] = dh.astype(bf16)
    sums[...] = jnp.zeros_like(sums)
    sums[0:1, :] = jnp.sum(dn * unit, axis=0, keepdims=True)
    sums[1:2, :] = jnp.sum(dn, axis=0, keepdims=True)
    sums[2:3, :] = jnp.sum(dh, axis=0, keepdims=True)
    sums[3:4, :] = jnp.sum(grad, axis=0, keepdims=True)


def back_two(h, dy, d0, dc, dx, gains):
    rows, dim = h.shape
    outs = [((rows, dim), f32), ((rows, dim), bf16), ((8, dim), f32)]
    return call(back_two_body, outs, [VM] * 6, [], "back_two", 1.5)(h, dy, d0, dc, dx, gains)


def attend_back_body(n_parts, last, *refs):
    meta, doc, q, k, v, kh, vh, ot, lse = refs[:9]
    ds_in = refs[9:11]
    parts = refs[11 : 11 + n_parts]
    rest = refs[11 + n_parts :]
    if last:
        before, (dq, dk, dv, dkh, dvh, qvsum, dhb, wbuf, ka, va, kha, vha) = rest[:5], rest[5:]
    else:
        dq, ka, va, kha, vha, dhb, wbuf = rest
    tp, side = meta[0], meta[1]
    total, width = q.shape
    rows = ds_in[0].shape[0]
    own_tiles = total // TILE
    wbuf = whole_weight(parts, wbuf, side)
    for j in range(2):
        dhb[pl.ds(j * rows, rows), :] = ds_in[j][...]
    masks = lane_masks()
    if last:
        for acc, old in zip((ka, va, kha, vha), before[1:]):
            acc[...] = old[...]
        for j in range(2):
            r = pl.ds(rows_of(tp, j, rows), rows)
            dq[r, :] = before[0][r, :]
    else:
        for acc in (ka, va, kha, vha):
            acc[...] = jnp.zeros_like(acc)

    def q_block(n, _):
        i = lax.bitwise_xor(tp, n + (2 if last else 0))
        r = pl.ds(pl.multiple_of(i * TILE, TILE), TILE)
        rd = pl.ds(pl.multiple_of(n * TILE, TILE), TILE)
        q_views = head_views(q[r, :], masks)
        doc_row = doc[0:1, r]
        grad = nt(dhb[rd, :], wbuf[...]).astype(bf16)
        grad_t = nt(wbuf[...], dhb[rd, :]).astype(bf16).astype(f32)
        inner = ot[:, r].astype(f32) * grad_t
        deltas = [
            jnp.sum(inner[h * HEAD : (h + 1) * HEAD, :], axis=0, keepdims=True) for h in range(3)
        ]
        logs = [lse[h : h + 1, r] for h in range(3)]
        g_views = head_views(grad, masks)

        def tile_step(jt, base, kk, vv, kacc, vacc, carry):
            rk = pl.ds(pl.multiple_of((jt - base) * TILE, TILE), TILE)
            dq_pair, dq_last = carry
            k_pair, k_last = kk[rk, 0:128], kk[rk, 128:192]
            v_pair, v_last = vv[rk, 0:128], vv[rk, 128:192]
            sides = scores_of(k_pair, k_last, q_views, allowed_in(jt, i, doc_row, own_tiles))
            grads = (nt(v_pair, g_views[0]), nt(v_pair, g_views[1]), nt(v_last, g_views[2]))
            ps = [jnp.exp(sides[h] - logs[h]) for h in range(3)]
            low = [p.astype(bf16) for p in ps]
            dss = [(ps[h] * (grads[h] - deltas[h])).astype(bf16) for h in range(3)]
            vacc[rk, 0:128] += nn(low[0], g_views[0]) + nn(low[1], g_views[1])
            vacc[rk, 128:192] += nn(low[2], g_views[2])
            kacc[rk, 0:128] += nn(dss[0], q_views[0]) + nn(dss[1], q_views[1])
            kacc[rk, 128:192] += nn(dss[2], q_views[2])
            dq_pair = dq_pair + tn(dss[0], k_pair * masks[0]) + tn(dss[1], k_pair * masks[1])
            dq_last = dq_last + tn(dss[2], k_last)
            return dq_pair, dq_last

        low_tile = meta[4 + i]
        carry = (jnp.zeros((TILE, 128), f32), jnp.zeros((TILE, HEAD), f32))
        carry = lax.fori_loop(
            low_tile, own_tiles, lambda jt, cc: tile_step(jt, 0, kh, vh, kha, vha, cc), carry
        )
        carry = lax.fori_loop(
            jnp.maximum(low_tile, own_tiles),
            own_tiles + i + 1,
            lambda jt, cc: tile_step(jt, own_tiles, k, v, ka, va, cc),
            carry,
        )
        dq[r, 0:128] = (carry[0] * 0.125).astype(bf16)
        dq[r, 128:192] = (carry[1] * 0.125).astype(bf16)
        return 0

    lax.fori_loop(0, 2, q_block, 0)
    if not last:
        return
    dk[...] = ka[...].astype(bf16)
    dv[...] = va[...].astype(bf16)
    dkh[...] = kha[...].astype(bf16)
    dvh[...] = vha[...].astype(bf16)
    qvsum[0:1, :] = jnp.sum(dq[...].astype(f32), axis=0, keepdims=True)
    qvsum[1:2, :] = jnp.sum(dv[...].astype(f32), axis=0, keepdims=True) + jnp.sum(
        dvh[...].astype(f32), axis=0, keepdims=True
    )


def attend_back(meta, doc, q, k, v, kh, vh, ot, lse, ds_in, parts, before=()):
    total, width = q.shape
    rows, dim = ds_in[0].shape
    last = len(before) > 0
    scratch = [pltpu.VMEM((2 * rows, dim), bf16), pltpu.VMEM((width, dim), bf16)]
    if last:
        outs = [((total, width), bf16)] * 5 + [((2, width), f32)]
        scratch += [pltpu.VMEM((total, width), f32)] * 4
    else:
        outs = [((total, width), bf16)] + [((total, width), f32)] * 4
    return call(
        partial(attend_back_body, len(parts), last),
        outs,
        [SM] + [VM] * (10 + len(parts) + len(before)),
        scratch,
        "attend_back",
        6,
    )(meta, doc, q, k, v, kh, vh, ot, lse, *ds_in, *parts, *before)


def attn_grads_kernel(split, meta, dq, dk, dv, dkh, dvh, n1, n1h, ot, *refs):
    ds_in, outs = refs[:4], refs[4:]
    picks = halves(meta[1], split, n1.shape[1])
    width = dv.shape[1]
    rows = ds_in[0].shape[0]
    for pick, out in list(zip(picks, outs))[::-1]:
        own, far = n1[:, pick], n1h[:, pick]
        out[0:width, :] = tn(dq[...], own).astype(bf16)
        out[width : 2 * width, :] = (tn(dk[...], own) + tn(dkh[...], far)).astype(bf16)
        out[2 * width : 3 * width, :] = (tn(dv[...], own) + tn(dvh[...], far)).astype(bf16)
        total = jnp.zeros((width, pick.size), f32)
        for j in range(4):
            r = pl.ds(rows_of(meta[0], j, rows), rows)
            total += nn(ot[:, r], ds_in[j][:, pick])
        out[3 * width :, :] = total.astype(bf16)


def attn_grads(meta, dq, dk, dv, dkh, dvh, n1, n1h, ot, ds_in, split):
    width, dim = dv.shape[1], n1.shape[1]
    n = 2 if split else 1
    outs = [((4 * width, dim // n), bf16)] * n
    return call(
        partial(attn_grads_kernel, split), outs, [SM] + [VM] * 12, [], "attn_grads", 4
    )(meta, dq, dk, dv, dkh, dvh, n1, n1h, ot, *ds_in)


def put_pair(ref, at, value):
    high = value.astype(bf16)
    ref[at : at + 8, :] = high
    ref[at + 8 : at + 16, :] = (value - high.astype(f32)).astype(bf16)


def take_pair(ref, at):
    value = ref[at : at + 8, :].astype(f32) + ref[at + 8 : at + 16, :].astype(f32)
    row = lax.broadcasted_iota(jnp.int32, value.shape, 0)
    return jnp.where(row < 6, value, 0.0)


def halo_mid_kernel(h2, got, sums, mid, sums_out):
    rows = h2.shape[0]
    mid[0:rows, :] = (h2[...].astype(f32) + got[0:rows, :].astype(f32)).astype(bf16)
    value = sums[...] + take_pair(got, rows)
    sums_out[...] = value
    put_pair(mid, rows, value)


def halo_mid(h2, got, sums):
    outs = [(got.shape, bf16), (sums.shape, f32)]
    return call(halo_mid_kernel, outs, [VM] * 3, [], "halo_mid", 0.5)(h2, got, sums)


def halo_end_kernel(h0, h1, got, sums, far, sums_out):
    rows = h0.shape[0]
    value = h0[...].astype(f32) + h1[...].astype(f32) + got[0:rows, :].astype(f32)
    far[...] = value.astype(bf16)
    sums_out[...] = sums[...] + take_pair(got, rows)


def halo_end(h0, h1, got, sums):
    outs = [(h0.shape, bf16), (sums.shape, f32)]
    return call(halo_end_kernel, outs, [VM] * 4, [], "halo_end", 0.5)(h0, h1, got, sums)


def own_mid_kernel(o2, o3, out):
    out[...] = (o2[...].astype(f32) + o3[...].astype(f32)).astype(bf16)


def own_mid(o2, o3):
    return call(own_mid_kernel, [(o2.shape, bf16)], [VM] * 2, [], "own_mid", 0.5)(o2, o3)[0]


def round_kernel(n_add, n_pick, *refs):
    meta = refs[0]
    ins, outs = refs[1 : 1 + 2 * (n_add + n_pick)], refs[1 + 2 * (n_add + n_pick) :]
    for i in range(n_add):
        total = ins[2 * i][...].astype(f32) + ins[2 * i + 1][...].astype(f32)
        outs[i][...] = total.astype(bf16)
    inner = (meta[2] == 1) | (meta[2] == 2)
    for i in range(n_add, n_add + n_pick):

        @pl.when(inner)
        def _():
            outs[i][...] = ins[2 * i][...].astype(f32)

        @pl.when(jnp.logical_not(inner))
        def _():
            outs[i][...] = ins[2 * i + 1][...].astype(f32)


def round_of(meta, adds, picks=(), us=0.5):
    flat = [one for pair in (*adds, *picks) for one in pair]
    outs = [(pair[0].shape, bf16) for pair in adds] + [(pair[0].shape, f32) for pair in picks]
    return call(
        partial(round_kernel, len(adds), len(picks)),
        outs,
        [SM] + [VM] * len(flat),
        [],
        "round",
        us,
    )(meta, *flat)


def last_kernel(meta, mine, got, qkv_out, out_out):
    inner = (meta[2] == 1) | (meta[2] == 2)
    rows = qkv_out.shape[0]

    @pl.when(inner)
    def _():
        qkv_out[...] = mine[0:rows, :].astype(f32)
        out_out[...] = mine[rows:, :].astype(f32)

    @pl.when(jnp.logical_not(inner))
    def _():
        qkv_out[...] = got[0:rows, :].astype(f32)
        out_out[...] = got[rows:, :].astype(f32)


def last_of(meta, mine, got):
    rows, dim = mine.shape
    outs = [((3 * rows // 4, dim), f32), ((rows // 4, dim), f32)]
    return call(last_kernel, outs, [SM] + [VM] * 2, [], "last", 0.5)(meta, mine, got)


def input_grads_kernel(n_parts, *refs):
    meta, dq, dk, dv, dkh, dvh, unit, unith, two, fcsum, fcsum_b, qvsum = refs[:12]
    parts = refs[12 : 12 + n_parts]
    o0, o2, h0, h2, near, h1, o1, o3, sums, wbuf = refs[12 + n_parts :]
    tp, side = meta[0], meta[1]
    wbuf = whole_weight(parts, wbuf, side)
    width = dq.shape[1]
    rows, dim = o0.shape
    gain_sum = jnp.zeros((1, dim), f32)
    bias_sum = jnp.zeros((1, dim), f32)
    wq, wk, wv = wbuf[0:width, :], wbuf[width : 2 * width, :], wbuf[2 * width :, :]
    far_outs = {0: h0, 1: h1, 2: h2, 3: near.at[0:rows]}
    own_outs = {0: o0, 1: o1, 2: o2, 3: o3}
    for j in range(4):
        r = pl.ds(rows_of(tp, j, rows), rows)
        far = nn(dkh[r, :], wk) + nn(dvh[r, :], wv)
        far_outs[j][...] = far.astype(bf16)
        gain_sum += jnp.sum(far * unith[r, :].astype(f32), axis=0, keepdims=True)
        bias_sum += jnp.sum(far, axis=0, keepdims=True)
        own = nn(dq[r, :], wq) + nn(dk[r, :], wk) + nn(dv[r, :], wv)
        own_outs[j][...] = own.astype(bf16)
        gain_sum += jnp.sum(own * unit[r, :].astype(f32), axis=0, keepdims=True)
        bias_sum += jnp.sum(own, axis=0, keepdims=True)
    sums[...] = two[...]
    sums[4:5, :] = gain_sum
    sums[5:6, :] = bias_sum
    sums[6:7, :] = fcsum[...] + fcsum_b[...]
    sums[7:8, 0:width] = qvsum[0:1, :]
    sums[7:8, 256 : 256 + width] = qvsum[1:2, :]
    put_pair(near, rows, sums[...])


def input_grads(meta, dq, dk, dv, dkh, dvh, unit, unith, two, fcsums, qvsum, parts):
    total, dim = unit.shape
    width = dq.shape[1]
    rows = total // 4
    outs = [((rows, dim), bf16)] * 4
    outs += [((rows + 16, dim), bf16)] + [((rows, dim), bf16)] * 3 + [((8, dim), f32)]
    return call(
        partial(input_grads_kernel, len(parts)),
        outs,
        [SM] + [VM] * (11 + len(parts)),
        [pltpu.VMEM((3 * width, dim), bf16)],
        "input_grads",
        5,
    )(meta, dq, dk, dv, dkh, dvh, unit, unith, two, *fcsums, qvsum, *parts)


def back_one_body(x, dh, o0, o1, far, halo, gains, out):
    dn = o0[...].astype(f32) + o1[...].astype(f32)
    dn = dn + far[...].astype(f32) + halo[...].astype(f32)
    gain = gains[0:1, :].astype(f32)
    _, unit, inverse = norm_rows(x[...].astype(f32), gain, 0.0)
    out[...] = (dh[...] + norm_back(dn, unit, inverse, gain)).astype(bf16)


def back_one(x, dh, o0, o1, far, halo, gains):
    rows, dim = x.shape
    return call(back_one_body, [((rows, dim), bf16)], [VM] * 7, [], "back_one", 1.5)(
        x, dh, o0, o1, far, halo, gains
    )[0]


def flip(value, axis, bit):
    size = lax.axis_size(axis)
    return lax.ppermute(value, axis, [(i, i ^ bit) for i in range(size)])


def after(value, *others):
    return lax.optimization_barrier((value,) + others)[0]


def gather_four(own):
    near = flip(own, "tp", 1)
    far = flip(own, "tp", 2)
    return [own, near, far, flip(far, "tp", 1)]


def add_low(a, b):
    return (a.astype(f32) + b.astype(f32)).astype(bf16)


def along(value, pairs):
    return lax.ppermute(value, "ctx", pairs)


def step_one(value):
    return along(value, [(0, 1), (3, 2)])


def step_two(value):
    return along(value, [(1, 2), (2, 1)])


def step_three(value):
    return along(value, [(1, 0), (2, 3)])


class Line:
    def __init__(self):
        self.last = None

    def __call__(self, step, first, *rest, also=()):
        waits = [one for one in (self.last, *also) if one is not None]
        out = step(after(first, *waits) if waits else first, *rest)
        self.last = out[0] if isinstance(out, (tuple, list)) else out
        return out


def per_device(
    hidden,
    latent,
    latent_mask,
    segment_ids,
    norm_gains,
    row_biases,
    qv_bias,
    fc_bias,
    w_qkv,
    w_out,
    w_fc,
    w_proj,
    cotangent,
):
    own_rows, dim = hidden.shape
    part_width = w_qkv.shape[1]
    hidden_here = w_fc.shape[0]
    row_count = 4 * own_rows
    split = lax.axis_size("fsdp") == 2
    tp, side, place = lax.axis_index("tp"), lax.axis_index("fsdp"), lax.axis_index("ctx")

    x = pick(latent_mask, latent, hidden)
    x_prev = lax.ppermute(x, "ctx", [(i, i + 1) for i in range(lax.axis_size("ctx") - 1)])

    def gathered(value, *late):
        value = after(value, *late)
        if split:
            return [value, flip(value, "fsdp", 1)]
        return [lax.all_gather(value, "fsdp", axis=1, tiled=True)]

    w_rows = w_qkv.reshape(3 * part_width, w_qkv.shape[2])
    qkv_parts = gathered(w_rows)
    x_far = flip(x, "tp", 2)
    xs = [x, flip(x, "tp", 1), x_far, flip(after(x_far, qkv_parts[-1]), "tp", 1)]

    ids = segment_ids[0]
    first_pos = place * row_count
    own_ids = lax.dynamic_slice_in_dim(ids, first_pos, row_count)
    docs = jnp.arange(32, dtype=jnp.int32)
    starts = jnp.sum((ids[None, :] < docs[:, None]).astype(jnp.int32), axis=1)
    doc_row = jnp.sum(
        jnp.where(own_ids[None, :] == docs[:, None], starts[:, None], 0), axis=0
    ) - (first_pos - row_count)
    doc = doc_row[None, :]
    lows = jnp.maximum(doc_row[::TILE], 0) // TILE
    meta = jnp.concatenate(
        [jnp.stack([tp, side, place, place]).astype(jnp.int32), lows.astype(jnp.int32)]
    )

    line = Line()
    n1, unit, q, k, v, vt = line(
        lambda m: project(False, m, norm_gains, row_biases, qv_bias, xs, qkv_parts),
        meta,
    )
    xh_far = flip(after(x_prev, xs[2]), "tp", 2)
    out_parts = gathered(w_out, qkv_parts[-1])
    xhs = [
        x_prev,
        flip(x_prev, "tp", 1),
        xh_far,
        flip(after(xh_far, n1, out_parts[-1]), "tp", 1),
    ]
    fc_parts = gathered(w_fc, out_parts[-1], n1)
    proj_parts = gathered(w_proj, fc_parts[-1])
    dy_far = flip(after(cotangent, xh_far), "tp", 2)
    n1h, unith, kh, vh, vth = line(
        lambda m: project(True, m, norm_gains, row_biases, qv_bias, xhs, qkv_parts), meta
    )
    a0, a1, a2, a3, ot, lse = line(
        lambda m: attend(m, doc, q, k, v, vt, kh, vh, vth, out_parts, dim), meta
    )
    a2 = line(add_low, a2, flip(after(a3, dy_far, fc_parts[-1]), "tp", 1))
    a_far = flip(a2, "tp", 2)
    h, n2 = line(
        lambda one: residual(x, one, flip(a1, "tp", 1), a_far, norm_gains, row_biases),
        a0,
        also=(proj_parts[-1],),
    )
    dys = [cotangent, flip(cotangent, "tp", 1), dy_far, flip(dy_far, "tp", 1)]
    n2_far = flip(n2, "tp", 2)
    n2s = [n2, flip(n2, "tp", 1)]
    fcb = fc_bias[None, :]
    d0, d1, act_a, du_a, fc_a = line(
        lambda m: ffn(m, fcb, n2s[:2], dys[:2], fc_parts, proj_parts), meta
    )
    n2s += [n2_far, flip(after(n2_far, d0), "tp", 1)]
    d2, d3, act_b, du_b, fc_b = line(
        lambda m: ffn(m, fcb, n2s[2:], dys[2:], fc_parts, proj_parts), meta
    )
    d2 = line(add_low, d2, flip(d3, "tp", 1))
    d_far = flip(d2, "tp", 2)
    tree = lax.axis_size("ctx") == 4 and split
    ga = line(lambda one: ffn_grad(meta, one, act_b, dys, split), act_a)
    got_a = flip(ga[1], "fsdp", 1) if split else None
    gb = line(lambda one: ffn_grad(meta, one, du_b, n2s, split), du_a)
    got_b = flip(gb[1], "fsdp", 1) if split else None
    y0, y1, y2, y3 = line(lambda one: ffn_out(meta, one, act_b, proj_parts), act_a)
    dh, dhb, sums_two = line(
        lambda one: back_two(h, cotangent, one, flip(d1, "tp", 1), d_far, norm_gains), d0
    )
    dh_far = flip(dhb, "tp", 2)
    dh_near = flip(dhb, "tp", 1)
    if tree:
        a_sum = line(lambda m: round_of(m, [(ga[0], got_a)], us=300)[0], meta)
        a_got = step_one(a_sum)
    back_a = line(
        lambda m: attend_back(m, doc, q, k, v, kh, vh, ot, lse, (dhb, dh_near), out_parts), meta
    )
    y2 = line(add_low, y2, flip(y3, "tp", 1))
    y_far = flip(after(y2, dh_far), "tp", 2)
    dhs = [dhb, dh_near, dh_far, flip(dh_far, "tp", 1)]
    dq, dk, dv, dkh, dvh, qv_sum = line(
        lambda m: attend_back(
            m, doc, q, k, v, kh, vh, ot, lse, dhs[2:], out_parts, tuple(back_a)
        ),
        meta,
    )
    if tree:
        a_sum, b_sum = line(lambda m: round_of(m, [(a_sum, a_got), (gb[0], got_b)]), meta)
        a_got, b_got = step_two(a_sum), step_one(b_sum)
    gc = line(
        lambda one: attn_grads(meta, one, dk, dv, dkh, dvh, n1, n1h, ot, dhs, split),
        dq,
        also=(y_far,),
    )
    got_c = flip(gc[1], "fsdp", 1) if split else None
    o0, o2, h0, h2, near, h1, o1, o3, sums = line(
        lambda one: input_grads(
            meta, one, dk, dv, dkh, dvh, unit, unith, sums_two, (fc_a, fc_b), qv_sum, qkv_parts
        ),
        dq,
    )
    near, h1, o1, o3 = (flip(one, "tp", 1) for one in (near, h1, o1, o3))

    def block_end(one):
        total = one.astype(f32) + flip(y1, "tp", 1).astype(f32) + y_far.astype(f32)
        return (h + total + row_biases[3].astype(f32)).astype(bf16)

    if tree:
        a_sum, b_sum = line(lambda m: round_of(m, [(a_sum, a_got), (b_sum, b_got)]), meta)
        a_got, b_got = step_three(a_sum), step_two(b_sum)
        c_sum = line(lambda m: round_of(m, [(gc[0], got_c)])[0], meta)
        c_got = step_one(c_sum)
    mid, sums = line(halo_mid, h2, near, sums)
    mid = flip(mid, "tp", 2)
    o2 = line(own_mid, o2, o3)
    o_far = flip(o2, "tp", 2)
    block_out = line(block_end, y0)
    if tree:
        b_sum, c_sum, shard_proj = line(
            lambda m: round_of(m, [(b_sum, b_got), (c_sum, c_got)], [(a_sum, a_got)]), meta
        )
        b_got, c_got = step_three(b_sum), step_two(c_sum)
    far, sums = line(halo_end, h0, h1, mid, sums)
    back = along(far, [(i + 1, i) for i in range(lax.axis_size("ctx") - 1)])
    if tree:
        got_sums = flip(sums, "fsdp", 1)
        sums = line(lambda one: one + got_sums, sums)
        near_sums, far_sums = flip(sums, "ctx", 1), (flip(sums, "ctx", 2), flip(sums, "ctx", 3))
        c_sum, shard_fc = line(
            lambda m: round_of(m, [(c_sum, c_got)], [(b_sum, b_got)]), meta
        )
        c_got = step_three(c_sum)
        grad_input = line(
            lambda one: back_one(one, dh, o0, o1, o_far, back, norm_gains), x
        )
        sums = line(lambda one: (one + near_sums) + (far_sums[0] + far_sums[1]), sums)
        shard_qkv, shard_out = line(lambda m: last_of(m, c_sum, c_got), meta)
    else:
        grad_input = back_one(x, dh, o0, o1, o_far, back, norm_gains)
        sums = lax.psum(sums, ("fsdp", "ctx"))
        shard_proj, shard_fc, shard_c = (
            lax.psum(
                lax.psum_scatter(one[0], "fsdp", scatter_dimension=1, tiled=True)
                if len(one) == 1
                else add_low(one[0], flip(one[1], "fsdp", 1)),
                "ctx",
            ).astype(f32)
            for one in (ga, gb, gc)
        )
        shard_qkv, shard_out = shard_c[: 3 * part_width], shard_c[3 * part_width :]

    small = lax.dynamic_slice_in_dim(sums[0:6], tp * part_width, part_width, 1)
    grad_gains = jnp.stack([small[4], small[0]])
    grad_biases = jnp.stack([small[5], small[1], small[2], small[3]])
    grad_qv = jnp.stack([sums[7, 0:part_width], sums[7, 256 : 256 + part_width]])
    grad_fcb = sums[6]
    return (
        block_out,
        grad_input,
        shard_qkv.reshape(3, part_width, -1),
        shard_out,
        shard_fc,
        shard_proj,
        grad_gains,
        grad_biases,
        grad_qv,
        grad_fcb,
    )


def solution(mesh):
    placed = (
        P(("fsdp", "ctx", "tp"), None),
        P(("fsdp", "ctx", "tp"), None),
        P(("fsdp", "ctx", "tp")),
        P("fsdp", None),
        P(),
        P(),
        P(None, "tp"),
        P("tp"),
        P(None, "tp", "fsdp"),
        P("tp", "fsdp"),
        P("tp", "fsdp"),
        P("tp", "fsdp"),
        P(("fsdp", "ctx", "tp"), None),
    )
    return jax.shard_map(
        per_device,
        mesh=mesh,
        in_specs=placed,
        out_specs=(
            P(("fsdp", "ctx", "tp"), None),
            P(("fsdp", "ctx", "tp"), None),
            P(None, "tp", "fsdp"),
            P("tp", "fsdp"),
            P("tp", "fsdp"),
            P("tp", "fsdp"),
            P(None, "tp"),
            P(None, "tp"),
            P(None, "tp"),
            P("tp"),
        ),
        check_vma=False,
    )
```

```python
from functools import partial

import jax
import jax.numpy as jnp
from jax import lax
from jax.experimental import pallas as pl
from jax.experimental.pallas import tpu as pltpu
from jax.sharding import PartitionSpec as P

HEAD = 64
TILE = 256
epsilon = 1e-05
masked_score = -1e30
f32 = jnp.float32
bf16 = jnp.bfloat16

VM = pl.BlockSpec(memory_space=pltpu.VMEM)
SM = pl.BlockSpec(memory_space=pltpu.SMEM)


def nn(a, b):
    return lax.dot_general(a, b, (((1,), (0,)), ((), ())), preferred_element_type=f32)


def nt(a, b):
    return lax.dot_general(a, b, (((1,), (1,)), ((), ())), preferred_element_type=f32)


def tn(a, b):
    return lax.dot_general(a, b, (((0,), (0,)), ((), ())), preferred_element_type=f32)


def call(body, outs, specs, scratch, name, us):
    return pl.pallas_call(
        body,
        out_shape=[jax.ShapeDtypeStruct(s, d) for s, d in outs],
        in_specs=specs,
        out_specs=[VM] * len(outs),
        scratch_shapes=scratch,
        name=name,
        compiler_params=pltpu.CompilerParams(vmem_limit_bytes=16 << 20),
        cost_estimate=pl.CostEstimate(
            flops=0, transcendentals=0, bytes_accessed=int(us * 3.0e4)
        ),
    )


def whole_weight(parts, dst, side):
    if len(parts) == 1:
        return parts[0]
    width = parts[0].shape[1]
    dst[:, pl.ds(pl.multiple_of(side * width, 128), width)] = parts[0][...]
    dst[:, pl.ds(pl.multiple_of((1 - side) * width, 128), width)] = parts[1][...]
    return dst


def norm_rows(values, gain, shift):
    mean = jnp.mean(values, axis=-1, keepdims=True)
    centered = values - mean
    variance = jnp.mean(centered * centered, axis=-1, keepdims=True)
    inverse = lax.rsqrt(variance + epsilon)
    unit = centered * inverse
    return unit * gain + shift, unit, inverse


def rows_of(tp, j, rows):
    return pl.multiple_of(lax.bitwise_xor(tp, j) * rows, rows)


def pick_kernel(mask, latent, hidden, out):
    for i in range(mask.shape[0]):
        column = jnp.transpose(jnp.broadcast_to(mask[i : i + 1, :], (128, 128)))[:, 0:1]
        r = slice(i * 128, (i + 1) * 128)
        chosen = jnp.where(column == 1, latent[r, :].astype(f32), hidden[r, :].astype(f32))
        out[r, :] = chosen.astype(bf16)


def pick(mask, latent, hidden):
    return call(pick_kernel, [(hidden.shape, bf16)], [VM] * 3, [], "pick", 0.5)(
        mask.reshape(-1, 128), latent, hidden
    )[0]


def project_body(n_parts, halo, *refs):
    meta, gains, biases, qvb = refs[:4]
    xs = refs[4:8]
    parts = refs[8 : 8 + n_parts]
    outs = refs[8 + n_parts :]
    if halo:
        n1, unit, k, v, vt, wbuf = outs
    else:
        n1, unit, q, k, v, vt, wbuf = outs
    width = k.shape[1]
    rows = xs[0].shape[0]
    tp, side = meta[0], meta[1]
    wbuf = whole_weight(parts, wbuf, side)
    gain = gains[0:1, :].astype(f32)
    shift = biases[0:1, :].astype(f32)
    bias_q = qvb[0:1, :].astype(f32)
    bias_v = qvb[1:2, :].astype(f32)
    bias_vt = jnp.transpose(jnp.broadcast_to(bias_v, (128, width)))[:, 0:1]
    for j in range(4):
        normed, unit_rows, _ = norm_rows(xs[j][...].astype(f32), gain, shift)
        low = normed.astype(bf16)
        r = pl.ds(rows_of(tp, j, rows), rows)
        n1[r, :] = low
        unit[r, :] = unit_rows.astype(bf16)
        if not halo:
            q[r, :] = ((nt(low, wbuf[0:width, :]) + bias_q).astype(bf16) * 0.125).astype(bf16)
        k[r, :] = nt(low, wbuf[width : 2 * width, :]).astype(bf16)
        v[r, :] = (nt(low, wbuf[2 * width :, :]) + bias_v).astype(bf16)
        vt[:, r] = (nt(wbuf[2 * width :, :], low) + bias_vt).astype(bf16)


def project(halo, meta, gains, biases, qvb, xs, parts):
    rows, dim = xs[0].shape
    width = parts[0].shape[0] // 3
    total = 4 * rows
    outs = [((total, dim), bf16), ((total, dim), bf16)]
    if not halo:
        outs.append(((total, width), bf16))
    outs += [((total, width), bf16), ((total, width), bf16), ((width, total), bf16)]
    return call(
        partial(project_body, len(parts), halo),
        outs,
        [SM, VM, VM, VM] + [VM] * (4 + len(parts)),
        [pltpu.VMEM((3 * width, dim), bf16)],
        "project_halo" if halo else "project_own",
        5,
    )(meta, gains, biases, qvb, *xs, *parts)


def lane_masks():
    lane = lax.broadcasted_iota(jnp.int32, (1, 128), 1)
    low = jnp.where(lane < HEAD, 1.0, 0.0).astype(bf16)
    return low, (1.0 - low.astype(f32)).astype(bf16)


def head_views(block, masks):
    pair = block[:, 0:128]
    return (pair * masks[0], pair * masks[1], block[:, 128:192])


def scores_of(k_pair, k_last, q_views, allowed):
    sides = (nt(k_pair, q_views[0]), nt(k_pair, q_views[1]), nt(k_last, q_views[2]))
    return [jnp.where(allowed, one, masked_score) for one in sides]


def allowed_in(jt, i, doc_row, own_tiles):
    key = jt * TILE + lax.broadcasted_iota(jnp.int32, (TILE, TILE), 0)
    query = (own_tiles + i) * TILE + lax.broadcasted_iota(jnp.int32, (1, TILE), 1)
    return (key >= doc_row) & (key <= query)


def attend_body(n_parts, *refs):
    meta, doc, q, k, v, vt, kh, vh, vth = refs[:9]
    parts = refs[9 : 9 + n_parts]
    a0, a1, a2, a3, ot, lse, wbuf = refs[9 + n_parts :]
    tp, side = meta[0], meta[1]
    total, width = q.shape
    own_tiles = total // TILE
    wbuf = whole_weight(parts, wbuf, side)
    masks = lane_masks()

    def q_block(i, _):
        r = pl.ds(pl.multiple_of(i * TILE, TILE), TILE)
        q_views = head_views(q[r, :], masks)
        doc_row = doc[0:1, r]
        start = (
            tuple(jnp.full((1, TILE), masked_score, f32) for _ in range(3)),
            tuple(jnp.zeros((1, TILE), f32) for _ in range(3)),
            tuple(jnp.zeros((HEAD, TILE), f32) for _ in range(3)),
        )

        def tile_step(jt, base, kk, vv, carry):
            rk = pl.ds(pl.multiple_of((jt - base) * TILE, TILE), TILE)
            highs, sums, accs = carry
            sides = scores_of(
                kk[rk, 0:128], kk[rk, 128:192], q_views, allowed_in(jt, i, doc_row, own_tiles)
            )
            new_h, new_s, new_a = [], [], []
            for h in range(3):
                high = jnp.maximum(highs[h], jnp.max(sides[h], axis=0, keepdims=True))
                shrink = jnp.exp(highs[h] - high)
                p = jnp.exp(sides[h] - high)
                new_h.append(high)
                new_s.append(sums[h] * shrink + jnp.sum(p, axis=0, keepdims=True))
                vv_h = vv[h * HEAD : (h + 1) * HEAD, rk]
                new_a.append(accs[h] * shrink + nn(vv_h, p.astype(bf16)))
            return tuple(new_h), tuple(new_s), tuple(new_a)

        low = meta[4 + i]
        carry = lax.fori_loop(
            low, own_tiles, lambda jt, cc: tile_step(jt, 0, kh, vth, cc), start
        )
        carry = lax.fori_loop(
            jnp.maximum(low, own_tiles),
            own_tiles + i + 1,
            lambda jt, cc: tile_step(jt, own_tiles, k, vt, cc),
            carry,
        )
        highs, sums, accs = carry
        for h in range(3):
            ot[h * HEAD : (h + 1) * HEAD, r] = (accs[h] / sums[h]).astype(bf16)
            lse[h : h + 1, r] = highs[h] + jnp.log(sums[h])
        return 0

    lax.fori_loop(0, own_tiles, q_block, 0)
    rows = a0.shape[0]
    for j, out in ((3, a3), (1, a1), (2, a2), (0, a0)):
        r = pl.ds(rows_of(tp, j, rows), rows)
        out[...] = tn(ot[:, r], wbuf[...]).astype(bf16)


def attend(meta, doc, q, k, v, vt, kh, vh, vth, parts, dim):
    total, width = q.shape
    rows = total // 4
    outs = [((rows, dim), bf16)] * 4 + [((width, total), bf16), ((8, total), f32)]
    return call(
        partial(attend_body, len(parts)),
        outs,
        [SM] + [VM] * 8 + [VM] * len(parts),
        [pltpu.VMEM((width, dim), bf16)],
        "attend",
        7,
    )(meta, doc, q, k, v, vt, kh, vh, vth, *parts)


def resid_body(x, a0, ac, ax, gains, biases, h_out, n2_out):
    h = (
        x[...].astype(f32)
        + (a0[...].astype(f32) + ac[...].astype(f32) + ax[...].astype(f32))
        + biases[2:3, :].astype(f32)
    )
    h_out[...] = h
    normed, _, _ = norm_rows(
        h.astype(bf16).astype(f32), gains[1:2, :].astype(f32), biases[1:2, :].astype(f32)
    )
    n2_out[...] = normed.astype(bf16)


def residual(x, a0, ac, ax, gains, biases):
    rows, dim = x.shape
    return call(
        resid_body, [((rows, dim), f32), ((rows, dim), bf16)], [VM] * 6, [], "residual", 1.5
    )(x, a0, ac, ax, gains, biases)


def ffn_kernel(n_parts, *refs):
    meta, fcb = refs[:2]
    n2s = refs[2:4]
    dys = refs[4:6]
    fcs = refs[6 : 6 + n_parts]
    projs = refs[6 + n_parts : 6 + 2 * n_parts]
    d0, d1, act, du, fcsum, fcw, pjw = refs[6 + 2 * n_parts :]
    side = meta[1]
    rows = n2s[0].shape[0]
    fcw = whole_weight(fcs, fcw, side)
    pjw = whole_weight(projs, pjw, side)
    bias = fcb[...].astype(f32)
    outs = (d0, d1)
    sums = jnp.zeros((1, fcw.shape[0]), f32)
    c0 = 0.7978845608028654
    c1 = 0.044715
    for j in (1, 0):
        r = pl.ds(j * rows, rows)
        u = nt(n2s[j][...], fcw[...]) + bias
        sq = u * u
        th = jnp.tanh(c0 * u * (1.0 + c1 * sq))
        half = 0.5 * (1.0 + th)
        act[r, :] = (u * half).astype(bf16)
        slope = half + (0.5 * c0) * u * (1.0 - th * th) * (1.0 + (3.0 * c1) * sq)
        grad = (nt(dys[j][...], pjw[...]) * slope).astype(bf16)
        du[r, :] = grad
        sums = sums + jnp.sum(grad.astype(f32), axis=0, keepdims=True)
        outs[j][...] = nn(grad, fcw[...]).astype(bf16)
    fcsum[...] = sums


def ffn(meta, fcb, n2s, dys, fcs, projs):
    rows, dim = n2s[0].shape
    hidden = fcs[0].shape[0]
    outs = [((rows, dim), bf16)] * 2
    outs += [((2 * rows, hidden), bf16)] * 2 + [((1, hidden), f32)]
    return call(
        partial(ffn_kernel, len(fcs)),
        outs,
        [SM, VM] + [VM] * (4 + 2 * len(fcs)),
        [pltpu.VMEM((hidden, dim), bf16), pltpu.VMEM((hidden, dim), bf16)],
        "ffn",
        4,
    )(meta, fcb, *n2s, *dys, *fcs, *projs)


def halves(side, split, width):
    if not split:
        return [pl.ds(0, width)]
    part = width // 2
    return [
        pl.ds(pl.multiple_of(side * part, 128), part),
        pl.ds(pl.multiple_of((1 - side) * part, 128), part),
    ]


def ffn_grad_kernel(split, meta, low, high, *refs):
    pieces, outs, right = refs[:4], refs[4:-1], refs[-1]
    picks = halves(meta[1], split, right.shape[1])
    rows = pieces[0].shape[0]
    for j in range(4):
        right[pl.ds(j * rows, rows), :] = pieces[j][...]
    for pick, out in zip(picks[::-1], outs[::-1]):
        total = tn(low[...], right[0 : 2 * rows, pick]) + tn(high[...], right[2 * rows :, pick])
        out[...] = total.astype(bf16)


def ffn_grad(meta, low, high, pieces, split):
    total, hidden = low.shape
    dim = pieces[0].shape[1]
    n = 2 if split else 1
    return call(
        partial(ffn_grad_kernel, split),
        [((hidden, dim // n), bf16)] * n,
        [SM] + [VM] * 6,
        [pltpu.VMEM((2 * total, dim), bf16)],
        "ffn_grad",
        3,
    )(meta, low, high, *pieces)


def ffn_out_kernel(n_parts, *refs):
    meta, low, high = refs[:3]
    parts = refs[3 : 3 + n_parts]
    outs = refs[3 + n_parts : 7 + n_parts]
    pjw = whole_weight(parts, refs[7 + n_parts], meta[1])
    rows = outs[0].shape[0]
    for j in range(4):
        act = high if j > 1 else low
        outs[j][...] = nn(act[pl.ds((j % 2) * rows, rows), :], pjw[...]).astype(bf16)


def ffn_out(meta, low, high, parts):
    total, hidden = low.shape
    dim = parts[0].shape[1] * len(parts)
    return call(
        partial(ffn_out_kernel, len(parts)),
        [((total // 2, dim), bf16)] * 4,
        [SM, VM, VM] + [VM] * len(parts),
        [pltpu.VMEM((hidden, dim), bf16)],
        "ffn_out",
        3,
    )(meta, low, high, *parts)


def norm_back(grad, unit, inverse, gain):
    g = grad * gain
    first = jnp.mean(g, axis=-1, keepdims=True)
    second = jnp.mean(g * unit, axis=-1, keepdims=True)
    return inverse * (g - first - unit * second)


def back_two_body(h, dy, d0, dc, dx, gains, dh_out, dhb_out, sums):
    dn = d0[...].astype(f32) + dc[...].astype(f32) + dx[...].astype(f32)
    gain = gains[1:2, :].astype(f32)
    _, unit, inverse = norm_rows(h[...].astype(bf16).astype(f32), gain, 0.0)
    grad = dy[...].astype(f32)
    dh = grad + norm_back(dn, unit, inverse, gain)
    dh_out[...] = dh
    dhb_out[...] = dh.astype(bf16)
    sums[...] = jnp.zeros_like(sums)
    sums[0:1, :] = jnp.sum(dn * unit, axis=0, keepdims=True)
    sums[1:2, :] = jnp.sum(dn, axis=0, keepdims=True)
    sums[2:3, :] = jnp.sum(dh, axis=0, keepdims=True)
    sums[3:4, :] = jnp.sum(grad, axis=0, keepdims=True)


def back_two(h, dy, d0, dc, dx, gains):
    rows, dim = h.shape
    outs = [((rows, dim), f32), ((rows, dim), bf16), ((8, dim), f32)]
    return call(back_two_body, outs, [VM] * 6, [], "back_two", 1.5)(h, dy, d0, dc, dx, gains)


def attend_back_body(n_parts, last, *refs):
    meta, doc, q, k, v, kh, vh, ot, lse = refs[:9]
    ds_in = refs[9:11]
    parts = refs[11 : 11 + n_parts]
    rest = refs[11 + n_parts :]
    if last:
        before, (dq, dk, dv, dkh, dvh, qvsum, dhb, wbuf, ka, va, kha, vha) = rest[:5], rest[5:]
    else:
        dq, ka, va, kha, vha, dhb, wbuf = rest
    tp, side = meta[0], meta[1]
    total, width = q.shape
    rows = ds_in[0].shape[0]
    own_tiles = total // TILE
    wbuf = whole_weight(parts, wbuf, side)
    for j in range(2):
        dhb[pl.ds(j * rows, rows), :] = ds_in[j][...]
    masks = lane_masks()
    if last:
        for acc, old in zip((ka, va, kha, vha), before[1:]):
            acc[...] = old[...]
        for j in range(2):
            r = pl.ds(rows_of(tp, j, rows), rows)
            dq[r, :] = before[0][r, :]
    else:
        for acc in (ka, va, kha, vha):
            acc[...] = jnp.zeros_like(acc)

    def q_block(n, _):
        i = lax.bitwise_xor(tp, n + (2 if last else 0))
        r = pl.ds(pl.multiple_of(i * TILE, TILE), TILE)
        rd = pl.ds(pl.multiple_of(n * TILE, TILE), TILE)
        q_views = head_views(q[r, :], masks)
        doc_row = doc[0:1, r]
        grad = nt(dhb[rd, :], wbuf[...]).astype(bf16)
        grad_t = nt(wbuf[...], dhb[rd, :]).astype(bf16).astype(f32)
        inner = ot[:, r].astype(f32) * grad_t
        deltas = [
            jnp.sum(inner[h * HEAD : (h + 1) * HEAD, :], axis=0, keepdims=True) for h in range(3)
        ]
        logs = [lse[h : h + 1, r] for h in range(3)]
        g_views = head_views(grad, masks)

        def tile_step(jt, base, kk, vv, kacc, vacc, carry):
            rk = pl.ds(pl.multiple_of((jt - base) * TILE, TILE), TILE)
            dq_pair, dq_last = carry
            k_pair, k_last = kk[rk, 0:128], kk[rk, 128:192]
            v_pair, v_last = vv[rk, 0:128], vv[rk, 128:192]
            sides = scores_of(k_pair, k_last, q_views, allowed_in(jt, i, doc_row, own_tiles))
            grads = (nt(v_pair, g_views[0]), nt(v_pair, g_views[1]), nt(v_last, g_views[2]))
            ps = [jnp.exp(sides[h] - logs[h]) for h in range(3)]
            low = [p.astype(bf16) for p in ps]
            dss = [(ps[h] * (grads[h] - deltas[h])).astype(bf16) for h in range(3)]
            vacc[rk, 0:128] += nn(low[0], g_views[0]) + nn(low[1], g_views[1])
            vacc[rk, 128:192] += nn(low[2], g_views[2])
            kacc[rk, 0:128] += nn(dss[0], q_views[0]) + nn(dss[1], q_views[1])
            kacc[rk, 128:192] += nn(dss[2], q_views[2])
            dq_pair = dq_pair + tn(dss[0], k_pair * masks[0]) + tn(dss[1], k_pair * masks[1])
            dq_last = dq_last + tn(dss[2], k_last)
            return dq_pair, dq_last

        low_tile = meta[4 + i]
        carry = (jnp.zeros((TILE, 128), f32), jnp.zeros((TILE, HEAD), f32))
        carry = lax.fori_loop(
            low_tile, own_tiles, lambda jt, cc: tile_step(jt, 0, kh, vh, kha, vha, cc), carry
        )
        carry = lax.fori_loop(
            jnp.maximum(low_tile, own_tiles),
            own_tiles + i + 1,
            lambda jt, cc: tile_step(jt, own_tiles, k, v, ka, va, cc),
            carry,
        )
        dq[r, 0:128] = (carry[0] * 0.125).astype(bf16)
        dq[r, 128:192] = (carry[1] * 0.125).astype(bf16)
        return 0

    lax.fori_loop(0, 2, q_block, 0)
    if not last:
        return
    dk[...] = ka[...].astype(bf16)
    dv[...] = va[...].astype(bf16)
    dkh[...] = kha[...].astype(bf16)
    dvh[...] = vha[...].astype(bf16)
    qvsum[0:1, :] = jnp.sum(dq[...].astype(f32), axis=0, keepdims=True)
    qvsum[1:2, :] = jnp.sum(dv[...].astype(f32), axis=0, keepdims=True) + jnp.sum(
        dvh[...].astype(f32), axis=0, keepdims=True
    )


def attend_back(meta, doc, q, k, v, kh, vh, ot, lse, ds_in, parts, before=()):
    total, width = q.shape
    rows, dim = ds_in[0].shape
    last = len(before) > 0
    scratch = [pltpu.VMEM((2 * rows, dim), bf16), pltpu.VMEM((width, dim), bf16)]
    if last:
        outs = [((total, width), bf16)] * 5 + [((2, width), f32)]
        scratch += [pltpu.VMEM((total, width), f32)] * 4
    else:
        outs = [((total, width), bf16)] + [((total, width), f32)] * 4
    return call(
        partial(attend_back_body, len(parts), last),
        outs,
        [SM] + [VM] * (10 + len(parts) + len(before)),
        scratch,
        "attend_back",
        6,
    )(meta, doc, q, k, v, kh, vh, ot, lse, *ds_in, *parts, *before)


def attn_grads_kernel(split, meta, dq, dk, dv, dkh, dvh, n1, n1h, ot, *refs):
    ds_in, outs = refs[:4], refs[4:]
    picks = halves(meta[1], split, n1.shape[1])
    width = dv.shape[1]
    rows = ds_in[0].shape[0]
    for pick, out in list(zip(picks, outs))[::-1]:
        own, far = n1[:, pick], n1h[:, pick]
        out[0:width, :] = tn(dq[...], own).astype(bf16)
        out[width : 2 * width, :] = (tn(dk[...], own) + tn(dkh[...], far)).astype(bf16)
        out[2 * width : 3 * width, :] = (tn(dv[...], own) + tn(dvh[...], far)).astype(bf16)
        total = jnp.zeros((width, pick.size), f32)
        for j in range(4):
            r = pl.ds(rows_of(meta[0], j, rows), rows)
            total += nn(ot[:, r], ds_in[j][:, pick])
        out[3 * width :, :] = total.astype(bf16)


def attn_grads(meta, dq, dk, dv, dkh, dvh, n1, n1h, ot, ds_in, split):
    width, dim = dv.shape[1], n1.shape[1]
    n = 2 if split else 1
    outs = [((4 * width, dim // n), bf16)] * n
    return call(
        partial(attn_grads_kernel, split), outs, [SM] + [VM] * 12, [], "attn_grads", 4
    )(meta, dq, dk, dv, dkh, dvh, n1, n1h, ot, *ds_in)


def put_pair(ref, at, value):
    high = value.astype(bf16)
    ref[at : at + 8, :] = high
    ref[at + 8 : at + 16, :] = (value - high.astype(f32)).astype(bf16)


def take_pair(ref, at):
    value = ref[at : at + 8, :].astype(f32) + ref[at + 8 : at + 16, :].astype(f32)
    row = lax.broadcasted_iota(jnp.int32, value.shape, 0)
    return jnp.where(row < 6, value, 0.0)


def halo_mid_kernel(h2, got, sums, mid, sums_out):
    rows = h2.shape[0]
    mid[0:rows, :] = (h2[...].astype(f32) + got[0:rows, :].astype(f32)).astype(bf16)
    value = sums[...] + take_pair(got, rows)
    sums_out[...] = value
    put_pair(mid, rows, value)


def halo_mid(h2, got, sums):
    outs = [(got.shape, bf16), (sums.shape, f32)]
    return call(halo_mid_kernel, outs, [VM] * 3, [], "halo_mid", 0.5)(h2, got, sums)


def halo_end_kernel(h0, h1, got, sums, far, sums_out):
    rows = h0.shape[0]
    value = h0[...].astype(f32) + h1[...].astype(f32) + got[0:rows, :].astype(f32)
    far[...] = value.astype(bf16)
    sums_out[...] = sums[...] + take_pair(got, rows)


def halo_end(h0, h1, got, sums):
    outs = [(h0.shape, bf16), (sums.shape, f32)]
    return call(halo_end_kernel, outs, [VM] * 4, [], "halo_end", 0.5)(h0, h1, got, sums)


def own_mid_kernel(o2, o3, out):
    out[...] = (o2[...].astype(f32) + o3[...].astype(f32)).astype(bf16)


def own_mid(o2, o3):
    return call(own_mid_kernel, [(o2.shape, bf16)], [VM] * 2, [], "own_mid", 0.5)(o2, o3)[0]


def round_kernel(n_add, n_pick, *refs):
    meta = refs[0]
    ins, outs = refs[1 : 1 + 2 * (n_add + n_pick)], refs[1 + 2 * (n_add + n_pick) :]
    for i in range(n_add):
        total = ins[2 * i][...].astype(f32) + ins[2 * i + 1][...].astype(f32)
        outs[i][...] = total.astype(bf16)
    inner = (meta[2] == 1) | (meta[2] == 2)
    for i in range(n_add, n_add + n_pick):

        @pl.when(inner)
        def _():
            outs[i][...] = ins[2 * i][...].astype(f32)

        @pl.when(jnp.logical_not(inner))
        def _():
            outs[i][...] = ins[2 * i + 1][...].astype(f32)


def round_of(meta, adds, picks=(), us=0.5):
    flat = [one for pair in (*adds, *picks) for one in pair]
    outs = [(pair[0].shape, bf16) for pair in adds] + [(pair[0].shape, f32) for pair in picks]
    return call(
        partial(round_kernel, len(adds), len(picks)),
        outs,
        [SM] + [VM] * len(flat),
        [],
        "round",
        us,
    )(meta, *flat)


def last_kernel(meta, mine, got, qkv_out, out_out):
    inner = (meta[2] == 1) | (meta[2] == 2)
    rows = qkv_out.shape[0]

    @pl.when(inner)
    def _():
        qkv_out[...] = mine[0:rows, :].astype(f32)
        out_out[...] = mine[rows:, :].astype(f32)

    @pl.when(jnp.logical_not(inner))
    def _():
        qkv_out[...] = got[0:rows, :].astype(f32)
        out_out[...] = got[rows:, :].astype(f32)


def last_of(meta, mine, got):
    rows, dim = mine.shape
    outs = [((3 * rows // 4, dim), f32), ((rows // 4, dim), f32)]
    return call(last_kernel, outs, [SM] + [VM] * 2, [], "last", 0.5)(meta, mine, got)


def small_grads_kernel(meta, own, one, two, three, gains, biases, qv, fcb):
    total = (own[...] + one[...]) + (two[...] + three[...])
    width = gains.shape[1]
    fcb[...] = total[6:7, :]
    qv[0:1, :] = total[7:8, 0:width]
    qv[1:2, :] = total[7:8, 256 : 256 + width]
    for t in range(total.shape[1] // width):

        @pl.when(meta[0] == t)
        def _():
            part = total[0:6, t * width : (t + 1) * width]
            gains[0:1, :] = part[4:5, :]
            gains[1:2, :] = part[0:1, :]
            biases[0:1, :] = part[5:6, :]
            biases[1:4, :] = part[1:4, :]


def small_grads(meta, own, others, width):
    shapes = [(2, width), (4, width), (2, width), (1, own.shape[1])]
    return call(
        small_grads_kernel, [(one, f32) for one in shapes], [SM] + [VM] * 4, [], "small_grads", 0.5
    )(meta, own, *others)


def input_grads_kernel(n_parts, *refs):
    meta, dq, dk, dv, dkh, dvh, unit, unith, two, fcsum, fcsum_b, qvsum = refs[:12]
    parts = refs[12 : 12 + n_parts]
    o0, o2, h0, h2, near, h1, o1, o3, sums, wbuf = refs[12 + n_parts :]
    tp, side = meta[0], meta[1]
    wbuf = whole_weight(parts, wbuf, side)
    width = dq.shape[1]
    rows, dim = o0.shape
    gain_sum = jnp.zeros((1, dim), f32)
    bias_sum = jnp.zeros((1, dim), f32)
    wq, wk, wv = wbuf[0:width, :], wbuf[width : 2 * width, :], wbuf[2 * width :, :]
    far_outs = {0: h0, 1: h1, 2: h2, 3: near.at[0:rows]}
    own_outs = {0: o0, 1: o1, 2: o2, 3: o3}
    for j in range(4):
        r = pl.ds(rows_of(tp, j, rows), rows)
        far = nn(dkh[r, :], wk) + nn(dvh[r, :], wv)
        far_outs[j][...] = far.astype(bf16)
        gain_sum += jnp.sum(far * unith[r, :].astype(f32), axis=0, keepdims=True)
        bias_sum += jnp.sum(far, axis=0, keepdims=True)
        own = nn(dq[r, :], wq) + nn(dk[r, :], wk) + nn(dv[r, :], wv)
        own_outs[j][...] = own.astype(bf16)
        gain_sum += jnp.sum(own * unit[r, :].astype(f32), axis=0, keepdims=True)
        bias_sum += jnp.sum(own, axis=0, keepdims=True)
    sums[...] = two[...]
    sums[4:5, :] = gain_sum
    sums[5:6, :] = bias_sum
    sums[6:7, :] = fcsum[...] + fcsum_b[...]
    sums[7:8, 0:width] = qvsum[0:1, :]
    sums[7:8, 256 : 256 + width] = qvsum[1:2, :]
    put_pair(near, rows, sums[...])


def input_grads(meta, dq, dk, dv, dkh, dvh, unit, unith, two, fcsums, qvsum, parts):
    total, dim = unit.shape
    width = dq.shape[1]
    rows = total // 4
    outs = [((rows, dim), bf16)] * 4
    outs += [((rows + 16, dim), bf16)] + [((rows, dim), bf16)] * 3 + [((8, dim), f32)]
    return call(
        partial(input_grads_kernel, len(parts)),
        outs,
        [SM] + [VM] * (11 + len(parts)),
        [pltpu.VMEM((3 * width, dim), bf16)],
        "input_grads",
        5,
    )(meta, dq, dk, dv, dkh, dvh, unit, unith, two, *fcsums, qvsum, *parts)


def back_one_body(x, dh, o0, o1, far, halo, gains, out):
    dn = o0[...].astype(f32) + o1[...].astype(f32)
    dn = dn + far[...].astype(f32) + halo[...].astype(f32)
    gain = gains[0:1, :].astype(f32)
    _, unit, inverse = norm_rows(x[...].astype(f32), gain, 0.0)
    out[...] = (dh[...] + norm_back(dn, unit, inverse, gain)).astype(bf16)


def back_one(x, dh, o0, o1, far, halo, gains):
    rows, dim = x.shape
    return call(back_one_body, [((rows, dim), bf16)], [VM] * 7, [], "back_one", 1.5)(
        x, dh, o0, o1, far, halo, gains
    )[0]


def flip(value, axis, bit):
    size = lax.axis_size(axis)
    return lax.ppermute(value, axis, [(i, i ^ bit) for i in range(size)])


def after(value, *others):
    return lax.optimization_barrier((value,) + others)[0]


def gather_four(own):
    near = flip(own, "tp", 1)
    far = flip(own, "tp", 2)
    return [own, near, far, flip(far, "tp", 1)]


def add_low(a, b):
    return (a.astype(f32) + b.astype(f32)).astype(bf16)


def along(value, pairs):
    return lax.ppermute(value, "ctx", pairs)


def step_one(value):
    return along(value, [(0, 1), (3, 2)])


def step_two(value):
    return along(value, [(1, 2), (2, 1)])


def step_three(value):
    return along(value, [(1, 0), (2, 3)])


class Line:
    def __init__(self):
        self.last = None

    def __call__(self, step, first, *rest, also=()):
        waits = [one for one in (self.last, *also) if one is not None]
        out = step(after(first, *waits) if waits else first, *rest)
        self.last = out[0] if isinstance(out, (tuple, list)) else out
        return out


def per_device(
    hidden,
    latent,
    latent_mask,
    segment_ids,
    norm_gains,
    row_biases,
    qv_bias,
    fc_bias,
    w_qkv,
    w_out,
    w_fc,
    w_proj,
    cotangent,
):
    own_rows, dim = hidden.shape
    part_width = w_qkv.shape[1]
    hidden_here = w_fc.shape[0]
    row_count = 4 * own_rows
    split = lax.axis_size("fsdp") == 2
    tp, side, place = lax.axis_index("tp"), lax.axis_index("fsdp"), lax.axis_index("ctx")

    x = pick(latent_mask, latent, hidden)
    x_prev = lax.ppermute(x, "ctx", [(i, i + 1) for i in range(lax.axis_size("ctx") - 1)])

    def gathered(value, *late):
        value = after(value, *late)
        if split:
            return [value, flip(value, "fsdp", 1)]
        return [lax.all_gather(value, "fsdp", axis=1, tiled=True)]

    w_rows = w_qkv.reshape(3 * part_width, w_qkv.shape[2])
    qkv_parts = gathered(w_rows)
    x_far = flip(x, "tp", 2)
    xs = [x, flip(x, "tp", 1), x_far, flip(after(x_far, qkv_parts[-1]), "tp", 1)]

    ids = segment_ids[0]
    first_pos = place * row_count
    own_ids = lax.dynamic_slice_in_dim(ids, first_pos, row_count)
    docs = jnp.arange(32, dtype=jnp.int32)
    starts = jnp.sum((ids[None, :] < docs[:, None]).astype(jnp.int32), axis=1)
    doc_row = jnp.sum(
        jnp.where(own_ids[None, :] == docs[:, None], starts[:, None], 0), axis=0
    ) - (first_pos - row_count)
    doc = doc_row[None, :]
    lows = jnp.maximum(doc_row[::TILE], 0) // TILE
    meta = jnp.concatenate(
        [jnp.stack([tp, side, place, place]).astype(jnp.int32), lows.astype(jnp.int32)]
    )

    line = Line()
    n1, unit, q, k, v, vt = line(
        lambda m: project(False, m, norm_gains, row_biases, qv_bias, xs, qkv_parts),
        meta,
    )
    xh_far = flip(after(x_prev, xs[2]), "tp", 2)
    out_parts = gathered(w_out, qkv_parts[-1])
    xhs = [
        x_prev,
        flip(x_prev, "tp", 1),
        xh_far,
        flip(after(xh_far, n1, out_parts[-1]), "tp", 1),
    ]
    fc_parts = gathered(w_fc, out_parts[-1], n1)
    proj_parts = gathered(w_proj, fc_parts[-1])
    dy_far = flip(after(cotangent, xh_far), "tp", 2)
    n1h, unith, kh, vh, vth = line(
        lambda m: project(True, m, norm_gains, row_biases, qv_bias, xhs, qkv_parts), meta
    )
    a0, a1, a2, a3, ot, lse = line(
        lambda m: attend(m, doc, q, k, v, vt, kh, vh, vth, out_parts, dim), meta
    )
    a2 = line(add_low, a2, flip(after(a3, dy_far, fc_parts[-1]), "tp", 1))
    a_far = flip(a2, "tp", 2)
    h, n2 = line(
        lambda one: residual(x, one, flip(a1, "tp", 1), a_far, norm_gains, row_biases),
        a0,
        also=(proj_parts[-1],),
    )
    dys = [cotangent, flip(cotangent, "tp", 1), dy_far, flip(dy_far, "tp", 1)]
    n2_far = flip(n2, "tp", 2)
    n2s = [n2, flip(n2, "tp", 1)]
    fcb = fc_bias[None, :]
    d0, d1, act_a, du_a, fc_a = line(
        lambda m: ffn(m, fcb, n2s[:2], dys[:2], fc_parts, proj_parts), meta
    )
    n2s += [n2_far, flip(after(n2_far, d0), "tp", 1)]
    d2, d3, act_b, du_b, fc_b = line(
        lambda m: ffn(m, fcb, n2s[2:], dys[2:], fc_parts, proj_parts), meta
    )
    d2 = line(add_low, d2, flip(d3, "tp", 1))
    d_far = flip(d2, "tp", 2)
    tree = lax.axis_size("ctx") == 4 and split
    ga = line(lambda one: ffn_grad(meta, one, act_b, dys, split), act_a)
    got_a = flip(ga[1], "fsdp", 1) if split else None
    gb = line(lambda one: ffn_grad(meta, one, du_b, n2s, split), du_a)
    got_b = flip(gb[1], "fsdp", 1) if split else None
    y0, y1, y2, y3 = line(lambda one: ffn_out(meta, one, act_b, proj_parts), act_a)
    dh, dhb, sums_two = line(
        lambda one: back_two(h, cotangent, one, flip(d1, "tp", 1), d_far, norm_gains), d0
    )
    dh_far = flip(dhb, "tp", 2)
    dh_near = flip(dhb, "tp", 1)
    if tree:
        a_sum = line(lambda m: round_of(m, [(ga[0], got_a)], us=300)[0], meta)
        a_got = step_one(a_sum)
    back_a = line(
        lambda m: attend_back(m, doc, q, k, v, kh, vh, ot, lse, (dhb, dh_near), out_parts), meta
    )
    y2 = line(add_low, y2, flip(y3, "tp", 1))
    y_far = flip(after(y2, dh_far), "tp", 2)
    dhs = [dhb, dh_near, dh_far, flip(dh_far, "tp", 1)]
    dq, dk, dv, dkh, dvh, qv_sum = line(
        lambda m: attend_back(
            m, doc, q, k, v, kh, vh, ot, lse, dhs[2:], out_parts, tuple(back_a)
        ),
        meta,
    )
    if tree:
        a_sum, b_sum = line(lambda m: round_of(m, [(a_sum, a_got), (gb[0], got_b)]), meta)
        a_got, b_got = step_two(a_sum), step_one(b_sum)
    gc = line(
        lambda one: attn_grads(meta, one, dk, dv, dkh, dvh, n1, n1h, ot, dhs, split),
        dq,
    )
    got_c = flip(gc[1], "fsdp", 1) if split else None
    o0, o2, h0, h2, near, h1, o1, o3, sums = line(
        lambda one: input_grads(
            meta, one, dk, dv, dkh, dvh, unit, unith, sums_two, (fc_a, fc_b), qv_sum, qkv_parts
        ),
        dq,
    )
    near, h1, o1, o3 = (flip(one, "tp", 1) for one in (near, h1, o1, o3))

    def block_end(one):
        total = one.astype(f32) + flip(y1, "tp", 1).astype(f32) + y_far.astype(f32)
        return (h + total + row_biases[3].astype(f32)).astype(bf16)

    if tree:
        a_sum = line(lambda m: round_of(m, [(a_sum, a_got)])[0], meta)
        a_got = step_three(a_sum)
        b_sum = line(lambda m: round_of(m, [(b_sum, b_got)])[0], meta)
        b_got = step_two(b_sum)
    mid, sums = line(halo_mid, h2, near, sums)
    mid = flip(mid, "tp", 2)
    o2 = line(own_mid, o2, o3)
    o_far = flip(o2, "tp", 2)
    if tree:
        c_sum = line(lambda m: round_of(m, [(gc[0], got_c)])[0], meta)
        c_got = step_one(c_sum)
    block_out = line(block_end, y0)
    far, sums = line(halo_end, h0, h1, mid, sums)
    back = along(far, [(i + 1, i) for i in range(lax.axis_size("ctx") - 1)])
    if tree:
        got_sums = flip(sums, "fsdp", 1)
        b_sum = line(lambda m: round_of(m, [(b_sum, b_got)])[0], meta, also=(a_got,))
        b_got = step_three(b_sum)
        c_sum = line(lambda m: round_of(m, [(c_sum, c_got)])[0], meta, also=(back, o_far, got_sums))
        c_got = step_two(c_sum)
        shard_proj = line(lambda m: round_of(m, [], [(a_sum, a_got)])[0], meta)
        grad_input = line(
            lambda one: back_one(one, dh, o0, o1, o_far, back, norm_gains), x
        )
        sums = line(lambda one: one + got_sums, sums)
        others = [flip(sums, "ctx", bit) for bit in (1, 2, 3)]
        c_sum = line(lambda m: round_of(m, [(c_sum, c_got)])[0], meta, also=(b_got,))
        c_got = step_three(c_sum)
        shard_fc = line(lambda m: round_of(m, [], [(b_sum, b_got)])[0], meta)
        shard_qkv, shard_out = line(lambda m: last_of(m, c_sum, c_got), meta)
        grad_gains, grad_biases, grad_qv, grad_fcb = line(
            lambda m: small_grads(m, sums, others, part_width), meta
        )
    else:
        grad_input = back_one(x, dh, o0, o1, o_far, back, norm_gains)
        sums = lax.psum(sums, ("fsdp", "ctx"))
        shard_proj, shard_fc, shard_c = (
            lax.psum(
                lax.psum_scatter(one[0], "fsdp", scatter_dimension=1, tiled=True)
                if len(one) == 1
                else add_low(one[0], flip(one[1], "fsdp", 1)),
                "ctx",
            ).astype(f32)
            for one in (ga, gb, gc)
        )
        shard_qkv, shard_out = shard_c[: 3 * part_width], shard_c[3 * part_width :]
        small = lax.dynamic_slice_in_dim(sums[0:6], tp * part_width, part_width, 1)
        grad_gains = jnp.stack([small[4], small[0]])
        grad_biases = jnp.stack([small[5], small[1], small[2], small[3]])
        grad_qv = jnp.stack([sums[7, 0:part_width], sums[7, 256 : 256 + part_width]])
        grad_fcb = sums[6]

    return (
        block_out,
        grad_input,
        shard_qkv.reshape(3, part_width, -1),
        shard_out,
        shard_fc,
        shard_proj,
        grad_gains,
        grad_biases,
        grad_qv,
        grad_fcb.reshape(-1),
    )


def solution(mesh):
    placed = (
        P(("fsdp", "ctx", "tp"), None),
        P(("fsdp", "ctx", "tp"), None),
        P(("fsdp", "ctx", "tp")),
        P("fsdp", None),
        P(),
        P(),
        P(None, "tp"),
        P("tp"),
        P(None, "tp", "fsdp"),
        P("tp", "fsdp"),
        P("tp", "fsdp"),
        P("tp", "fsdp"),
        P(("fsdp", "ctx", "tp"), None),
    )
    return jax.shard_map(
        per_device,
        mesh=mesh,
        in_specs=placed,
        out_specs=(
            P(("fsdp", "ctx", "tp"), None),
            P(("fsdp", "ctx", "tp"), None),
            P(None, "tp", "fsdp"),
            P("tp", "fsdp"),
            P("tp", "fsdp"),
            P("tp", "fsdp"),
            P(None, "tp"),
            P(None, "tp"),
            P(None, "tp"),
            P("tp"),
        ),
        check_vma=False,
    )
```
